256 devices in a mesh: src: 16 (over z_lo, y), rcv: 16 (over z_hi, x, core).
Axes of the slice: x: 4, y: 4, z: 8 (z_hi: 2, z_lo: 4; z = z_hi * 4 + z_lo), core: 2. Of those that a mesh axis runs over, the one named last changes fastest.
Arguments:
- records: bfloat16 [4096, 8192], P(('rcv', 'src')), may hold values from -6 to 6
- live_mask: int32 [4096], P(('rcv', 'src')), may hold values 0 or 1
- offsets: int32 [64], replicated, may hold values from 0 to 7936
- block_ids: int32 [2, 16], P(None, 'src'), may hold values from 0 to 31
Outputs:
- stacked: bfloat16 [2, 76, 2048, 4096], P(None, None, 'src', 'rcv')
The draws below stay inside these ranges and needn't reach their ends.
All inputs are finite; a program needn't handle non-finite values. No bound on the sum of `live_mask` on one device may be relied on, other than what follows from the above.
Results may differ from the reference program's by a relative error of at most 0.0059.
Values may be sent and summed in bfloat16 or wider, within the bound.
A program may use at most 128 MiB of HBM per device.

```python
import jax
import jax.numpy as jnp
from jax import lax

NW = 64
NT = 8192
L = 256
SB = 128
LAGS = 76
TURNS = 2
C = 4096
BLOCKS = 32
N_SRC = 16


def set_ends(array, own_key, least, high):
    spot = [jax.random.randint(jax.random.fold_in(own_key, axis), (), 0, length) for axis, length in enumerate(array.shape)]
    widest = array.shape.index(max(array.shape))
    neighbour = spot[:widest] + [(spot[widest] + 1) % array.shape[widest]] + spot[widest + 1:]
    return array.at[tuple(spot)].set(least).at[tuple(neighbour)].set(high)


def levels(own_key, shape, pieces, smallest, high):
    gain, own = 1.0, jax.random.fold_in(own_key, 6)
    for axis_at, parts in pieces:
        heights = jnp.exp(jax.random.uniform(jax.random.fold_in(own, axis_at), (parts,), jnp.float32, smallest / len(pieces), high / len(pieces)))
        gain = gain * jnp.repeat(heights, shape[axis_at] // parts).reshape([-1 if axis == axis_at else 1 for axis in range(len(shape))])
    return gain


def bell_draw(key, dims, width, most, shards=(), kind=jnp.bfloat16):
    loudness = levels(key, dims, shards, -0.22, 0.18) if shards else 1.0
    drawn = jax.random.normal(key, dims, jnp.float32) * width * loudness
    return jnp.minimum(jnp.maximum(drawn, -most), most).astype(kind)


def setup_inputs(seed: int = 0) -> dict:
    splits = jax.random.split(jax.random.key(seed), 5)
    return {
        "records": bell_draw(splits[0], (C, NT), 1.0, 6.0, ((0, 256),)),
        "live_mask": set_ends((jax.random.randint(splits[1], (C,), 0, 16) < 15).astype(jnp.int32), jax.random.fold_in(splits[1], 1), 0, 1),
        "offsets": set_ends(jax.random.randint(splits[2], (NW,), 0, NT - L + 1), jax.random.fold_in(splits[2], 1), 0, NT - L).astype(jnp.int32),
        "block_ids": set_ends(jax.random.randint(splits[3], (TURNS, N_SRC), 0, BLOCKS), jax.random.fold_in(splits[3], 1), 0, BLOCKS - 1).astype(jnp.int32),
    }


def build_tables(length, win_count, lag_count):
    sample_axis = jnp.arange(length, dtype=jnp.float32)
    bin_count = length // 2
    bin_axis = jnp.arange(bin_count, dtype=jnp.float32)
    phases = 2.0 * jnp.pi * sample_axis[:, None] * bin_axis[None, :] / length
    taper = 0.5 - 0.5 * jnp.cos(2.0 * jnp.pi * sample_axis / length)
    dft_table = jnp.concatenate([taper[:, None] * jnp.cos(phases), -taper[:, None] * jnp.sin(phases)], axis=1).astype(jnp.bfloat16)
    lag_axis = jnp.arange(lag_count, dtype=jnp.float32)
    weights = jnp.where(bin_axis == 0, 1.0, 2.0).astype(jnp.float32)
    lag_table = (weights[:, None] * jnp.cos(2.0 * jnp.pi * bin_axis[:, None] * lag_axis[None, :] / length) * (2.0 / (win_count * length))).astype(jnp.bfloat16)
    return dft_table, lag_table


def transform(live_rec, offsets, dft_table):
    receiver_total = live_rec.shape[0]
    length = dft_table.shape[0]
    win_count = offsets.shape[0]
    windows = jax.vmap(lambda anchor: lax.dynamic_slice_in_dim(live_rec, anchor, length, 1))(offsets)
    flat_spec = jnp.dot(windows.reshape(win_count * receiver_total, length), dft_table, preferred_element_type=jnp.float32).astype(jnp.bfloat16)
    bin_count = dft_table.shape[1] // 2
    return flat_spec.reshape(win_count, receiver_total, 2, bin_count).transpose(3, 1, 2, 0).reshape(bin_count, receiver_total, 2 * win_count)


def correlate(source_block, receiver_block, lag_table, src_chan, rcv_chan):
    cross_spectrum = jnp.einsum("mdt,mpt->mdp", source_block.astype(jnp.float32), receiver_block.astype(jnp.float32)).astype(jnp.bfloat16)
    bin_count, src_count, receiver_total = cross_spectrum.shape
    mixed = jnp.dot(lag_table.T, cross_spectrum.reshape(bin_count, src_count * receiver_total), preferred_element_type=jnp.float32)
    mixed = mixed.reshape(-1, src_count, receiver_total)
    self_pair = src_chan[:, None] == rcv_chan[None, :]
    return jnp.where(self_pair[None], 0.0, mixed).astype(jnp.bfloat16)


def reference(records, live_mask, offsets, block_ids):
    dft_table, lag_table = build_tables(L, NW, LAGS)
    live_rec = records * live_mask[:, None].astype(records.dtype)
    spectra = transform(live_rec, offsets, dft_table)
    all_chan = jnp.arange(C, dtype=jnp.int32)

    def one_block(block_id):
        begin = (block_id * SB).astype(jnp.int32)
        source_block = lax.dynamic_slice_in_dim(spectra, begin, SB, 1)
        src_chan = begin + jnp.arange(SB, dtype=jnp.int32)
        return correlate(source_block, spectra, lag_table, src_chan, all_chan)

    results = lax.map(one_block, block_ids.reshape(-1))
    results = results.reshape(TURNS, N_SRC, LAGS, SB, C).transpose(0, 2, 1, 3, 4)
    return results.reshape(TURNS, LAGS, N_SRC * SB, C)
```

```python
import functools

import jax
import jax.numpy as jnp
import numpy as np
from jax import lax
from jax.experimental import pallas as pl
from jax.experimental.pallas import tpu as pltpu
from jax.sharding import PartitionSpec as P

L = 256
SB = 128
LAGS = 76
LAGP = 80
BINS = L // 2
LANES = 128
SPAN = L + LANES
STRIDE = 128
GROUP = 16


def tables(win_count):
    sample_axis = np.arange(L, dtype=np.float32)
    bin_axis = np.arange(BINS, dtype=np.float32)
    two_pi = np.float32(2.0 * np.pi)
    phases = two_pi * sample_axis[:, None] * bin_axis[None, :] / np.float32(L)
    taper = np.float32(0.5) - np.float32(0.5) * np.cos(two_pi * sample_axis / np.float32(L))
    dft = np.concatenate([taper[:, None] * np.cos(phases), -taper[:, None] * np.sin(phases)], axis=1)
    dft = dft.astype(jnp.bfloat16).astype(np.float32)
    shifted = np.zeros((L, SPAN), np.float32)
    shifted[:, :L] = dft.T
    lag_axis = np.arange(LAGS, dtype=np.float32)
    weights = np.where(bin_axis == 0, 1.0, 2.0).astype(np.float32)
    lag = (
        weights[:, None]
        * np.cos(two_pi * bin_axis[:, None] * lag_axis[None, :] / np.float32(L))
        * np.float32(2.0 / (win_count * L))
    )
    lag_t = np.zeros((LAGP, BINS), np.float32)
    lag_t[:LAGS] = lag.T
    return shifted, lag_t.astype(jnp.bfloat16)


def compute_kernel(off_ref, chan_ref, dft_ref, lag_ref, rcv_ref, src_ref, out_ref,
                   spec_rcv, spec_src, wide, lagged):
    turn, group = pl.program_id(0), pl.program_id(1)
    win_count = off_ref.shape[0]
    taps = 2 * win_count
    last = rcv_ref.shape[1] // LANES - SPAN // LANES

    def spectra(records_ref, store):
        @pl.loop(0, win_count)
        def _(w):
            first = off_ref[w]
            base = jnp.minimum(first // LANES, last)
            table = pltpu.roll(dft_ref[...], first - base * LANES, 1).astype(jnp.bfloat16)
            samples = records_ref[:, pl.ds(pl.multiple_of(base * LANES, LANES), SPAN)]
            value = lax.dot_general(table, samples, (((1,), (1,)), ((), ())),
                                    preferred_element_type=jnp.float32)
            for half in range(2):
                for part in range(2):
                    wide[half, pl.ds(part * win_count + w, BINS, stride=STRIDE), :] = (
                        value[part * BINS:(part + 1) * BINS, half * LANES:(half + 1) * LANES])

        @pl.loop(0, BINS)
        def _(f):
            for half in range(2):
                rows = wide[half, pl.ds(pl.multiple_of(f * STRIDE, 8), taps), :]
                store(f, half, rows.astype(jnp.bfloat16))

    @pl.when((turn == 0) & (group == 0))
    def _():
        def to_rcv(f, half, rows):
            spec_rcv[f, :, half * LANES:(half + 1) * LANES] = rows

        def to_src(f, half, rows):
            spec_src[half, f] = rows

        spectra(rcv_ref, to_rcv)
        spectra(src_ref, to_src)

    @pl.when(group == 0)
    def _():
        @pl.loop(0, BINS, unroll=2)
        def _(f):
            value = lax.dot_general(spec_src[turn, f], spec_rcv[f], (((0,), (0,)), ((), ())),
                                    preferred_element_type=jnp.float32)
            for half in range(2):
                wide[half, pl.ds(f, SB, stride=STRIDE), :] = value[:, half * LANES:(half + 1) * LANES]

    for s in range(GROUP):
        begin = pl.multiple_of((group * GROUP + s) * STRIDE, 8)
        for half in range(2):
            pass
        cross = jnp.concatenate(
            [wide[half, pl.ds(begin, BINS), :].astype(jnp.bfloat16) for half in range(2)], axis=1)
        value = jnp.dot(lag_ref[...], cross, preferred_element_type=jnp.float32)
        for half in range(2):
            lagged[half, pl.ds(s, LAGP, stride=GROUP), :] = value[:, half * LANES:(half + 1) * LANES]
    src_chan = chan_ref[turn] + group * GROUP + lax.broadcasted_iota(jnp.int32, (GROUP, LANES), 0)
    for half in range(2):
        rcv_chan = chan_ref[2] + half * LANES + lax.broadcasted_iota(jnp.int32, (GROUP, LANES), 1)
        apart = src_chan != rcv_chan
        for lag in range(LAGS):
            value = lagged[half, lag * GROUP:(lag + 1) * GROUP, :]
            out_ref[0, lag, :, half * LANES:(half + 1) * LANES] = (
                jnp.where(apart, value, 0.0).astype(jnp.bfloat16))


def compute(offsets, chans, rcv, src):
    win_count = offsets.shape[0]
    turns = src.shape[0] // SB
    rcv_total = rcv.shape[0]
    dft, lag = tables(win_count)
    taps = 2 * win_count
    whole = lambda shape: pl.BlockSpec(shape, lambda t, g, *_: (0,) * len(shape), pipeline_mode=pl.Buffered(1))
    return pl.pallas_call(
        compute_kernel,
        name="correlate",
        grid_spec=pltpu.PrefetchScalarGridSpec(
            num_scalar_prefetch=2,
            grid=(turns, SB // GROUP),
            in_specs=[whole(dft.shape), whole(lag.shape), whole(rcv.shape), whole(src.shape)],
            out_specs=pl.BlockSpec((1, LAGS, GROUP, rcv_total), lambda t, g, *_: (t, 0, g, 0)),
            scratch_shapes=[
                pltpu.VMEM((BINS, taps, rcv_total), jnp.bfloat16),
                pltpu.VMEM((turns, BINS, taps, SB), jnp.bfloat16),
                pltpu.VMEM((2, BINS * STRIDE, LANES), jnp.float32),
                pltpu.VMEM((2, LAGP * GROUP, LANES), jnp.float32),
            ],
        ),
        out_shape=jax.ShapeDtypeStruct((turns, LAGS, SB, rcv_total), jnp.bfloat16),
        compiler_params=pltpu.CompilerParams(vmem_limit_bytes=56 * 1024 * 1024),
    )(offsets, chans, dft, lag, rcv, src)


def local(records, live_mask, offsets, block_ids):
    members = records.shape[0] * lax.axis_size("src")
    live_rec = records * live_mask[:, None].astype(records.dtype)
    rcv = lax.all_gather(live_rec, "src", axis=0, tiled=True)
    first = block_ids[:, 0] * SB
    group = lax.axis_index("rcv")
    pieces = []
    for turn in range(block_ids.shape[0]):
        piece = lax.dynamic_slice_in_dim(rcv, first[turn] % members, SB, 0)
        pieces.append(jnp.where(first[turn] // members == group, piece, 0).astype(piece.dtype))
    src = lax.psum(jnp.concatenate(pieces), "rcv")
    chans = jnp.concatenate([first, (group * members)[None].astype(jnp.int32)])
    return compute(offsets, chans, rcv, src)


def solution(mesh):
    in_specs = (P(("rcv", "src"), None), P(("rcv", "src")), P(), P(None, "src"))
    out_specs = P(None, None, "src", "rcv")
    return jax.shard_map(local, mesh=mesh, in_specs=in_specs, out_specs=out_specs, check_vma=False)
```

```python
import jax
import jax.numpy as jnp
import numpy as np
from jax import lax
from jax.experimental import pallas as pl
from jax.experimental.pallas import tpu as pltpu
from jax.sharding import PartitionSpec as P

L = 256
SB = 128
LAGS = 76
LAGP = 80
BINS = L // 2
LANES = 128
SPAN = L + LANES
STRIDE = 136
GROUP = 16


def tables(win_count):
    sample_axis = np.arange(L, dtype=np.float32)
    bin_axis = np.arange(BINS, dtype=np.float32)
    two_pi = np.float32(2.0 * np.pi)
    phases = two_pi * sample_axis[:, None] * bin_axis[None, :] / np.float32(L)
    taper = np.float32(0.5) - np.float32(0.5) * np.cos(two_pi * sample_axis / np.float32(L))
    dft = np.concatenate([taper[:, None] * np.cos(phases), -taper[:, None] * np.sin(phases)], axis=1)
    dft = dft.astype(jnp.bfloat16).astype(np.float32)
    shifted = np.zeros((L, SPAN), np.float32)
    shifted[:, :L] = dft.T
    lag_axis = np.arange(LAGS, dtype=np.float32)
    weights = np.where(bin_axis == 0, 1.0, 2.0).astype(np.float32)
    lag = (
        weights[:, None]
        * np.cos(two_pi * bin_axis[:, None] * lag_axis[None, :] / np.float32(L))
        * np.float32(2.0 / (win_count * L))
    )
    lag_t = np.zeros((LAGP, BINS), np.float32)
    lag_t[:LAGS] = lag.T
    return shifted, lag_t.astype(jnp.bfloat16)


def compute_kernel(off_ref, chan_ref, dft_ref, lag_ref, rcv_ref, src_ref, out_ref,
                   spec_rcv, spec_src, wide, lagged):
    turn, group = pl.program_id(0), pl.program_id(1)
    win_count = off_ref.shape[0]
    taps = 2 * win_count
    last = rcv_ref.shape[1] // LANES - SPAN // LANES

    def spectra(records_ref, store):
        @pl.loop(0, win_count)
        def _(w):
            first = off_ref[w]
            base = jnp.minimum(first // LANES, last)
            table = pltpu.roll(dft_ref[...], first - base * LANES, 1).astype(jnp.bfloat16)
            samples = records_ref[:, pl.ds(pl.multiple_of(base * LANES, LANES), SPAN)]
            value = lax.dot_general(table, samples, (((1,), (1,)), ((), ())),
                                    preferred_element_type=jnp.float32)
            for half in range(2):
                for part in range(2):
                    wide[half, pl.ds(part * win_count + w, BINS, stride=STRIDE), :] = (
                        value[part * BINS:(part + 1) * BINS, half * LANES:(half + 1) * LANES])

        @pl.loop(0, BINS)
        def _(f):
            for half in range(2):
                rows = wide[half, pl.ds(pl.multiple_of(f * STRIDE, 8), taps), :]
                store(f, half, rows.astype(jnp.bfloat16))

    @pl.when((turn == 0) & (group == 0))
    def _():
        def to_rcv(f, half, rows):
            spec_rcv[f, :, half * LANES:(half + 1) * LANES] = rows

        def to_src(f, half, rows):
            spec_src[half, f] = rows

        spectra(rcv_ref, to_rcv)
        spectra(src_ref, to_src)

    @pl.when(group == 0)
    def _():
        @pl.loop(0, BINS, unroll=2)
        def _(f):
            value = lax.dot_general(spec_src[turn, f], spec_rcv[f], (((0,), (0,)), ((), ())),
                                    preferred_element_type=jnp.float32)
            for half in range(2):
                wide[half, pl.ds(f, SB, stride=STRIDE), :] = value[:, half * LANES:(half + 1) * LANES]

    for s in range(GROUP):
        begin = pl.multiple_of((group * GROUP + s) * STRIDE, 8)
        cross = jnp.concatenate(
            [wide[half, pl.ds(begin, BINS), :].astype(jnp.bfloat16) for half in range(2)], axis=1)
        value = jnp.dot(lag_ref[...], cross, preferred_element_type=jnp.float32)
        for half in range(2):
            lagged[half, pl.ds(s, LAGP, stride=GROUP), :] = value[:, half * LANES:(half + 1) * LANES]
    src_chan = chan_ref[turn] + group * GROUP + lax.broadcasted_iota(jnp.int32, (GROUP, LANES), 0)
    for half in range(2):
        rcv_chan = chan_ref[2] + half * LANES + lax.broadcasted_iota(jnp.int32, (GROUP, LANES), 1)
        apart = src_chan != rcv_chan
        for lag in range(LAGS):
            value = lagged[half, lag * GROUP:(lag + 1) * GROUP, :]
            out_ref[0, lag, :, half * LANES:(half + 1) * LANES] = (
                jnp.where(apart, value, 0.0).astype(jnp.bfloat16))


def compute(offsets, chans, rcv, src):
    win_count = offsets.shape[0]
    turns = src.shape[0] // SB
    rcv_total = rcv.shape[0]
    dft, lag = tables(win_count)
    taps = 2 * win_count
    whole = lambda shape: pl.BlockSpec(shape, lambda t, g, *_: (0,) * len(shape), pipeline_mode=pl.Buffered(1))
    return pl.pallas_call(
        compute_kernel,
        name="correlate",
        grid_spec=pltpu.PrefetchScalarGridSpec(
            num_scalar_prefetch=2,
            grid=(turns, SB // GROUP),
            in_specs=[whole(dft.shape), whole(lag.shape), whole(rcv.shape), whole(src.shape)],
            out_specs=pl.BlockSpec((1, LAGS, GROUP, rcv_total), lambda t, g, *_: (t, 0, g, 0)),
            scratch_shapes=[
                pltpu.VMEM((BINS, taps, rcv_total), jnp.bfloat16),
                pltpu.VMEM((turns, BINS, taps, SB), jnp.bfloat16),
                pltpu.VMEM((2, BINS * STRIDE, LANES), jnp.float32),
                pltpu.VMEM((2, LAGP * GROUP, LANES), jnp.float32),
            ],
        ),
        out_shape=jax.ShapeDtypeStruct((turns, LAGS, SB, rcv_total), jnp.bfloat16),
        compiler_params=pltpu.CompilerParams(vmem_limit_bytes=56 * 1024 * 1024),
    )(offsets, chans, dft, lag, rcv, src)


NX, NY, NZ, NC = 4, 4, 8, 2
ZL = NZ // 2
PIECES = 2
MESH = pl.DeviceIdType.MESH


def gather_kernel(rec_ref, live_ref, ids_ref, rcv_ref, src_ref, *scratch):
    columns = scratch[:PIECES]
    picked = scratch[PIECES:2 * PIECES]
    offered = scratch[2 * PIECES:3 * PIECES]
    chosen = scratch[3 * PIECES:4 * PIECES]
    merged = scratch[4 * PIECES:5 * PIECES]
    (id_buf, id_smem, z_send, z_recv, c_send, c_recv, x_send, x_recv, y_send, y_recv,
     g_send, g_recv, e_send, e_recv, r_send, r_recv, f_send, f_recv, i_send, i_recv,
     local_sem) = scratch[5 * PIECES:]
    shard, total = rec_ref.shape
    width = total // PIECES
    part = width // NX

    src, rcv = lax.axis_index("src"), lax.axis_index("rcv")
    y, zl = src % NY, src // NY
    core, x, zh = rcv % NC, (rcv // NC) % NX, rcv // (NC * NX)
    z = zh * ZL + zl

    def device(x_to=x, y_to=y, z_to=z, core_to=core):
        return {"src": (z_to % ZL) * NY + y_to,
                "rcv": ((z_to // ZL) * NX + x_to) * NC + core_to}

    def send(src_ref, dst_ref, send_sem, recv_sem, to):
        copy = pltpu.make_async_remote_copy(
            src_ref=src_ref, dst_ref=dst_ref, send_sem=send_sem, recv_sem=recv_sem,
            device_id=to, device_id_type=MESH)
        copy.start()
        return copy

    z_up, z_down = (z + 1) % NZ, (z + NZ - 1) % NZ
    sibling = device(core_to=1 - core)

    barrier = pltpu.get_barrier_semaphore()
    peers = [device(z_to=z_up), device(z_to=z_down), sibling]
    peers += [device(x_to=(x + d) % NX) for d in range(1, NX)]
    peers += [device(y_to=(y + d) % NY) for d in range(1, NY)]
    for peer in peers:
        pl.semaphore_signal(barrier, inc=1, device_id=peer, device_id_type=MESH)

    live = live_ref[:, :1]
    for t in range(PIECES):
        columns[t][core, z] = rec_ref[:, t * width:(t + 1) * width] * live
    id_buf[y] = ids_ref[...]
    pl.semaphore_wait(barrier, len(peers))

    started = []
    ids = [send(ids_ref, id_buf.at[y], i_send.at[d - 1], i_recv.at[d - 1],
                device(y_to=(y + d) % NY)) for d in range(1, NY)]

    def z_hop(t, way, hop):
        slot = (z - (hop - 1) + NZ) % NZ if way == 0 else (z + (hop - 1)) % NZ
        return send(columns[t].at[core, slot], columns[t].at[core, slot],
                    z_send.at[t, way, hop - 1], z_recv.at[t, way, hop - 1],
                    device(z_to=z_up if way == 0 else z_down))

    def to_sibling(t, slot, index):
        return send(columns[t].at[core, slot], columns[t].at[core, slot],
                    c_send.at[t, index], c_recv.at[t, index], sibling)

    hops = [(4, 3) if t % 2 == 0 else (3, 4) for t in range(PIECES)]
    flying = {}
    shared = [[] for _ in range(PIECES)]
    for t in range(PIECES):
        for way in range(2):
            flying[t, way] = z_hop(t, way, 1)
        shared[t].append(to_sibling(t, z, 0))
    for hop in range(1, NZ // 2 + 1):
        for t in range(PIECES):
            for way in range(2):
                if hop > hops[t][way]:
                    continue
                flying[t, way].wait_recv()
                started.append(flying[t, way])
                if hop < hops[t][way]:
                    flying[t, way] = z_hop(t, way, hop + 1)
                slot = (z - hop + NZ) % NZ if way == 0 else (z + hop) % NZ
                shared[t].append(to_sibling(t, slot, hop + way * hops[t][0]))

    for copy in ids:
        copy.wait()
    to_smem = pltpu.make_async_copy(id_buf, id_smem, local_sem.at[0])
    to_smem.start()
    to_smem.wait()

    def columns_span(t):
        return pl.ds(t * width, width)

    ring, mine, exchanged, spread, gathered, twins = [], [], [], [], [], []
    for t in range(PIECES):
        own = columns[t].at[core, pl.ds(zh * ZL, ZL)]
        target = rcv_ref.at[:, y, :, columns_span(t)]
        ring.append([send(own, target, r_send.at[t, way], r_recv.at[t, way],
                          device(y_to=(y + (1 if way == 0 else NY - 1)) % NY)) for way in range(2)])
        copy = pltpu.make_async_copy(own, target, local_sem.at[1 + t])
        copy.start()
        mine.append(copy)

        for copy in shared[t]:
            copy.wait_recv()
        started += shared[t]
        for y_of in range(NY):
            block = id_smem[y_of, core, 0]
            group = block // 2
            slot = (group // (NC * NX)) * ZL + (block % 2) * 2
            for p in range(2):
                for q in range(NX):
                    picked[t][q, y_of, p] = columns[t][group % NC, slot + p, :, q * part:(q + 1) * part]
        exchanged.append([send(picked[t].at[(x + d) % NX], offered[t].at[x], x_send.at[t, d - 1],
                               x_recv.at[t, d - 1], device(x_to=(x + d) % NX)) for d in range(1, NX)])
        offered[t][x] = picked[t][x]

    forward = []
    for t in range(PIECES):
        for copy in exchanged[t]:
            copy.wait_recv()
        started += exchanged[t]
        for y_of in range(NY):
            group = id_smem[y_of, core, 0] // 2
            chosen[t][y_of] = offered[t][(group // NC) % NX, y_of]
        spread.append([send(chosen[t].at[(y + d) % NY], merged[t].at[:, y], y_send.at[t, d - 1],
                            y_recv.at[t, d - 1], device(y_to=(y + d) % NY)) for d in range(1, NY)])
        for p in range(2):
            merged[t][p, y] = chosen[t][y, p]
        way = t % 2
        ring[t][way].wait_recv()
        from_y = (y + NY - 1) % NY if way == 0 else (y + 1) % NY
        to_y = (y + 1) % NY if way == 0 else (y + NY - 1) % NY
        forward.append(send(rcv_ref.at[:, from_y, :, columns_span(t)],
                            rcv_ref.at[:, from_y, :, columns_span(t)],
                            f_send.at[t], f_recv.at[t], device(y_to=to_y)))

    for t in range(PIECES):
        for copy in spread[t]:
            copy.wait_recv()
        started += spread[t]
        place = src_ref.at[core, :, :, :, pl.ds(t * width + x * part, part)]
        gathered.append([send(merged[t], place, g_send.at[t, d - 1], g_recv.at[t, d - 1],
                              device(x_to=(x + d) % NX)) for d in range(1, NX)])
        copy = pltpu.make_async_copy(merged[t], place, local_sem.at[1 + PIECES + t])
        copy.start()
        mine.append(copy)

    for t in range(PIECES):
        for copy in gathered[t]:
            copy.wait_recv()
        started += gathered[t]
        mine[PIECES + t].wait()
        whole = src_ref.at[core, :, :, :, columns_span(t)]
        twins.append(send(whole, whole, e_send.at[t], e_recv.at[t], sibling))

    for t in range(PIECES):
        mine[t].wait()
        ring[t][1 - t % 2].wait_recv()
        forward[t].wait_recv()
        twins[t].wait_recv()
        for copy in ring[t] + [forward[t], twins[t]]:
            copy.wait_send()
    for copy in started:
        copy.wait_send()


def gather(records, live_mask, block_ids):
    shard, total = records.shape
    width = total // PIECES
    turns = block_ids.shape[0]
    live = jnp.broadcast_to(live_mask[:, None].astype(records.dtype), (shard, LANES))
    ids = jnp.zeros((8, LANES), jnp.int32).at[:turns].set(block_ids)
    dma = pltpu.SemaphoreType.DMA
    vmem = pl.BlockSpec(memory_space=pltpu.VMEM)
    part = width // NX
    rcv, src = pl.pallas_call(
        gather_kernel,
        name="gather",
        in_specs=[vmem] * 3,
        out_specs=[vmem] * 2,
        out_shape=[
            jax.ShapeDtypeStruct((ZL, NY, shard, total), records.dtype),
            jax.ShapeDtypeStruct((turns, 2, NY, shard, total), records.dtype),
        ],
        scratch_shapes=(
            [pltpu.VMEM((NC, NZ, shard, width), records.dtype)] * PIECES
            + [pltpu.VMEM((NX, NY, 2, shard, part), records.dtype)] * (2 * PIECES)
            + [pltpu.VMEM((NY, 2, shard, part), records.dtype)] * PIECES
            + [pltpu.VMEM((2, NY, shard, part), records.dtype)] * PIECES
            + [
                pltpu.VMEM((NY, 8, LANES), jnp.int32),
                pltpu.SMEM((NY, 8, LANES), jnp.int32),
                dma((PIECES, 2, 4)), dma((PIECES, 2, 4)),
                dma((PIECES, NZ)), dma((PIECES, NZ)),
                dma((PIECES, 3)), dma((PIECES, 3)),
                dma((PIECES, 3)), dma((PIECES, 3)),
                dma((PIECES, 3)), dma((PIECES, 3)),
                dma((PIECES,)), dma((PIECES,)),
                dma((PIECES, 2)), dma((PIECES, 2)),
                dma((PIECES,)), dma((PIECES,)),
                dma((3,)), dma((3,)),
                dma((1 + 2 * PIECES,)),
            ]
        ),
        compiler_params=pltpu.CompilerParams(
            collective_id=0, has_side_effects=True, vmem_limit_bytes=40 * 1024 * 1024),
    )(records, live, ids)
    return rcv.reshape(-1, total), src.reshape(-1, total)


def local(records, live_mask, offsets, block_ids):
    members = records.shape[0] * lax.axis_size("src")
    rcv, src = gather(records, live_mask, block_ids)
    first = block_ids[:, 0] * SB
    group = lax.axis_index("rcv")
    chans = jnp.concatenate([first, (group * members)[None].astype(jnp.int32)])
    return compute(offsets, chans, rcv, src)


def solution(mesh):
    in_specs = (P(("rcv", "src"), None), P(("rcv", "src")), P(), P(None, "src"))
    out_specs = P(None, None, "src", "rcv")
    return jax.shard_map(local, mesh=mesh, in_specs=in_specs, out_specs=out_specs, check_vma=False)
```

```python
import jax
import jax.numpy as jnp
import numpy as np
from jax import lax
from jax.experimental import pallas as pl
from jax.experimental.pallas import tpu as pltpu
from jax.sharding import PartitionSpec as P

L = 256
SB = 128
LAGS = 76
LAGP = 80
BINS = L // 2
LANES = 128
SPAN = L + LANES
STRIDE = 132
GROUP = 32
ROWS = 36


def tables(win_count):
    sample_axis = np.arange(L, dtype=np.float32)
    bin_axis = np.arange(BINS, dtype=np.float32)
    two_pi = np.float32(2.0 * np.pi)
    phases = two_pi * sample_axis[:, None] * bin_axis[None, :] / np.float32(L)
    taper = np.float32(0.5) - np.float32(0.5) * np.cos(two_pi * sample_axis / np.float32(L))
    dft = np.concatenate([taper[:, None] * np.cos(phases), -taper[:, None] * np.sin(phases)], axis=1)
    dft = dft.astype(jnp.bfloat16).astype(np.float32)
    shifted = np.zeros((L, SPAN), np.float32)
    shifted[:, :L] = dft.T
    lag_axis = np.arange(LAGS, dtype=np.float32)
    weights = np.where(bin_axis == 0, 1.0, 2.0).astype(np.float32)
    lag = (
        weights[:, None]
        * np.cos(two_pi * bin_axis[:, None] * lag_axis[None, :] / np.float32(L))
        * np.float32(2.0 / (win_count * L))
    )
    lag_t = np.zeros((LAGP, BINS), np.float32)
    lag_t[:LAGS] = lag.T
    return shifted, lag_t.astype(jnp.bfloat16)


def compute_kernel(off_ref, chan_ref, dft_ref, lag_ref, rcv_ref, src_ref, out_ref,
                   spec_rcv, spec_src, wide, lagged):
    turn, group = pl.program_id(0), pl.program_id(1)
    win_count = off_ref.shape[0]
    taps = 2 * win_count
    last = rcv_ref.shape[1] // LANES - SPAN // LANES

    def spectra(records_ref, store):
        @pl.loop(0, win_count, unroll=8)
        def _(w):
            first = off_ref[w]
            base = jnp.minimum(first // LANES, last)
            table = pltpu.roll(dft_ref[...], first - base * LANES, 1).astype(jnp.bfloat16)
            samples = records_ref[:, pl.ds(pl.multiple_of(base * LANES, LANES), SPAN)]
            value = lax.dot_general(table, samples, (((1,), (1,)), ((), ())),
                                    preferred_element_type=jnp.float32)
            for half in range(2):
                for part in range(2):
                    wide[half, pl.ds(part * win_count + w, BINS, stride=STRIDE), :] = (
                        value[part * BINS:(part + 1) * BINS, half * LANES:(half + 1) * LANES])

        @pl.loop(0, BINS, unroll=8)
        def _(f):
            for half in range(2):
                rows = wide[half, pl.ds(pl.multiple_of(f * STRIDE, 4), taps), :]
                store(f, half, rows.astype(jnp.bfloat16))

    @pl.when((turn == 0) & (group == 0))
    def _():
        def to_rcv(f, half, rows):
            spec_rcv[f, :, half * LANES:(half + 1) * LANES] = rows

        def to_src(f, half, rows):
            spec_src[half, f] = rows

        spectra(rcv_ref, to_rcv)
        spectra(src_ref, to_src)

    @pl.when(group == 0)
    def _():
        @pl.loop(0, BINS, unroll=8)
        def _(f):
            value = lax.dot_general(spec_src[turn, f], spec_rcv[f], (((0,), (0,)), ((), ())),
                                    preferred_element_type=jnp.float32)
            for half in range(2):
                wide[half, pl.ds(f, SB, stride=STRIDE), :] = value[:, half * LANES:(half + 1) * LANES]

    for s in range(GROUP):
        begin = pl.multiple_of((group * GROUP + s) * STRIDE, 4)
        cross = jnp.concatenate(
            [wide[half, pl.ds(begin, BINS), :].astype(jnp.bfloat16) for half in range(2)], axis=1)
        value = jnp.dot(lag_ref[...], cross, preferred_element_type=jnp.float32)
        for half in range(2):
            lagged[half, pl.ds(s, LAGP, stride=ROWS), :] = value[:, half * LANES:(half + 1) * LANES]
    src_chan = chan_ref[turn] + group * GROUP + lax.broadcasted_iota(jnp.int32, (GROUP, LANES), 0)
    for half in range(2):
        rcv_chan = chan_ref[2] + half * LANES + lax.broadcasted_iota(jnp.int32, (GROUP, LANES), 1)
        apart = src_chan != rcv_chan
        for lag in range(LAGS):
            value = lagged[half, lag * ROWS:lag * ROWS + GROUP, :]
            out_ref[0, lag, :, half * LANES:(half + 1) * LANES] = (
                jnp.where(apart, value, 0.0).astype(jnp.bfloat16))


def compute(offsets, chans, rcv, src):
    win_count = offsets.shape[0]
    turns = src.shape[0] // SB
    rcv_total = rcv.shape[0]
    dft, lag = tables(win_count)
    taps = 2 * win_count
    whole = lambda shape: pl.BlockSpec(shape, lambda t, g, *_: (0,) * len(shape), pipeline_mode=pl.Buffered(1))
    return pl.pallas_call(
        compute_kernel,
        name="correlate",
        grid_spec=pltpu.PrefetchScalarGridSpec(
            num_scalar_prefetch=2,
            grid=(turns, SB // GROUP),
            in_specs=[whole(dft.shape), whole(lag.shape), whole(rcv.shape), whole(src.shape)],
            out_specs=pl.BlockSpec((1, LAGS, GROUP, rcv_total), lambda t, g, *_: (t, 0, g, 0)),
            scratch_shapes=[
                pltpu.VMEM((BINS, taps, rcv_total), jnp.bfloat16),
                pltpu.VMEM((turns, BINS, taps, SB), jnp.bfloat16),
                pltpu.VMEM((2, BINS * STRIDE, LANES), jnp.float32),
                pltpu.VMEM((2, LAGP * ROWS, LANES), jnp.float32),
            ],
        ),
        out_shape=jax.ShapeDtypeStruct((turns, LAGS, SB, rcv_total), jnp.bfloat16),
        compiler_params=pltpu.CompilerParams(vmem_limit_bytes=56 * 1024 * 1024),
    )(offsets, chans, dft, lag, rcv, src)


NX, NY, NZ, NC = 4, 4, 8, 2
ZL = NZ // 2
PIECES = 4
SKEW = 1
MESH = pl.DeviceIdType.MESH


def gather_kernel(rec_ref, live_ref, ids_ref, rcv_ref, src_ref, *scratch):
    columns, first, mixed, second, landed, chosen, merged = (
        scratch[i * PIECES:(i + 1) * PIECES] for i in range(7))
    (id_buf, id_smem, z_send, z_recv, c_send, c_recv, x_send, x_recv, y_send, y_recv,
     g_send, g_recv, e_send, e_recv, r_send, r_recv, i_send, i_recv,
     local_sem) = scratch[7 * PIECES:]
    shard, total = rec_ref.shape
    width = total // PIECES
    part = width // NX
    half = part // 2

    src, rcv = lax.axis_index("src"), lax.axis_index("rcv")
    y, zl = src % NY, src // NY
    core, x, zh = rcv % NC, (rcv // NC) % NX, rcv // (NC * NX)
    z = zh * ZL + zl

    def device(x_to=x, y_to=y, z_to=z, core_to=core):
        return {"src": (z_to % ZL) * NY + y_to,
                "rcv": ((z_to // ZL) * NX + x_to) * NC + core_to}

    sent = []

    def send(src_ref, dst_ref, send_sem, recv_sem, to):
        copy = pltpu.make_async_remote_copy(
            src_ref=src_ref, dst_ref=dst_ref, send_sem=send_sem, recv_sem=recv_sem,
            device_id=to, device_id_type=MESH)
        copy.start()
        sent.append(copy)
        return copy

    def step(position, way, count):
        return (position + 1) % count if way == 0 else (position + count - 1) % count

    sibling = device(core_to=1 - core)
    barrier = pltpu.get_barrier_semaphore()
    peers = [device(z_to=step(z, way, NZ)) for way in range(2)] + [sibling]
    peers += [device(x_to=step(x, way, NX)) for way in range(2)]
    peers += [device(y_to=(y + d) % NY) for d in range(1, NY)]
    for peer in peers:
        pl.semaphore_signal(barrier, inc=1, device_id=peer, device_id_type=MESH)

    live = live_ref[:, :1]
    for t in range(PIECES):
        columns[t][core, z] = rec_ref[:, t * width:(t + 1) * width] * live
    id_buf[y] = ids_ref[...]
    pl.semaphore_wait(barrier, len(peers))

    ids = [send(ids_ref, id_buf.at[y], i_send.at[d - 1], i_recv.at[d - 1],
                device(y_to=(y + d) % NY)) for d in range(1, NY)]

    def ids_ready():
        for copy in ids:
            copy.wait_recv()
        to_smem = pltpu.make_async_copy(id_buf, id_smem, local_sem.at[0])
        to_smem.start()
        to_smem.wait()

    locals_started = []

    def piece(t):
        hops = (4, 3) if t % 2 == 0 else (3, 4)
        lanes = pl.ds(t * width, width)
        flying, shared = {}, []
        state = {}

        def hop_send(way, hop):
            slot = (z - (hop - 1) + NZ) % NZ if way == 0 else (z + (hop - 1)) % NZ
            flying[way] = send(columns[t].at[core, slot], columns[t].at[core, slot],
                               z_send.at[t, way, hop - 1], z_recv.at[t, way, hop - 1],
                               device(z_to=step(z, way, NZ)))

        def share(slot, index):
            shared.append(send(columns[t].at[core, slot], columns[t].at[core, slot],
                               c_send.at[t, index], c_recv.at[t, index], sibling))

        def begin():
            for way in range(2):
                hop_send(way, 1)
            share(z, 0)

        def hop_stage(hop):
            def run():
                for way in range(2):
                    if hop <= hops[way]:
                        flying[way].wait_recv()
                        if hop < hops[way]:
                            hop_send(way, hop + 1)
                        share((z - hop + NZ) % NZ if way == 0 else (z + hop) % NZ, hop + way * hops[0])
            return run

        def receivers():
            own = columns[t].at[core, pl.ds(zh * ZL, ZL)]
            target = rcv_ref.at[:, y, :, lanes]
            state["ring"] = [send(own, target, r_send.at[t, way], r_recv.at[t, way],
                                  device(y_to=step(y, way, NY))) for way in range(2)]
            copy = pltpu.make_async_copy(own, target, local_sem.at[1 + t])
            copy.start()
            locals_started.append(copy)

        def receivers_on():
            way = t % 2
            state["ring"][way].wait_recv()
            held = rcv_ref.at[:, step(y, 1 - way, NY), :, lanes]
            state["on"] = send(held, held, r_send.at[t, 2], r_recv.at[t, 2], device(y_to=step(y, way, NY)))

        def pick():
            if t == 0:
                ids_ready()
            for copy in shared:
                copy.wait_recv()

            for y_of in range(NY):
                block = id_smem[y_of, core, 0]
                group = block // 2
                slot = (group // (NC * NX)) * ZL + (block % 2) * 2
                for p in range(2):
                    def take(q, h):
                        start = pl.multiple_of(q * part + h * half, half)
                        return columns[t][group % NC, slot + p, :, pl.ds(start, half)]

                    for h in range(2):
                        first[t][h, y_of, p] = take((x + 2) % NX, h)
                        landed[t][4 + h, y_of, p] = take(x, h)
                        mixed[t][h, 0, y_of, p] = take(step(x, h, NX), h)
                        second[t][h, 1, y_of, p] = take(step(x, h, NX), 1 - h)
            state["x1"] = [send(first[t].at[way], mixed[t].at[way, 1], x_send.at[t, way], x_recv.at[t, way],
                                device(x_to=step(x, way, NX))) for way in range(2)]

        def blend():
            for copy in state["x1"]:
                copy.wait_recv()
            state["x2"] = []
            for way in range(2):
                for y_of in range(NY):
                    root = (id_smem[y_of, core, 0] // (2 * NC)) % NX
                    other = jnp.where(root == step(x, 1 - way, NX), 1, 0)
                    second[t][way, 0, y_of] = mixed[t][way, other, y_of]
                state["x2"].append(send(second[t].at[way], landed[t].at[pl.ds(2 * way, 2)],
                                        x_send.at[t, 2 + way], x_recv.at[t, 2 + way],
                                        device(x_to=step(x, way, NX))))

        def choose():
            for copy in state["x2"]:
                copy.wait_recv()
            for y_of in range(NY):
                root = (id_smem[y_of, core, 0] // (2 * NC)) % NX
                away = (root - x + NX) % NX
                low = jnp.where(away == 0, 4, jnp.where(away == 1, 3, 0))
                high = jnp.where(away == 0, 5, jnp.where(away == 3, 1, 2))
                chosen[t][y_of, :, :, :half] = landed[t][low, y_of]
                chosen[t][y_of, :, :, half:] = landed[t][high, y_of]
            state["y"] = [send(chosen[t].at[(y + d) % NY], merged[t].at[:, y], y_send.at[t, d - 1],
                               y_recv.at[t, d - 1], device(y_to=(y + d) % NY)) for d in range(1, NY)]
            for p in range(2):
                merged[t][p, y] = chosen[t][y, p]

        def spread():
            for copy in state["y"]:
                copy.wait_recv()
            place = src_ref.at[core, :, :, :, pl.ds(t * width + x * part, part)]
            state["g1"] = [send(merged[t], place, g_send.at[t, way], g_recv.at[t, way],
                                device(x_to=step(x, way, NX))) for way in range(2)]
            copy = pltpu.make_async_copy(merged[t], place, local_sem.at[1 + PIECES + t])
            copy.start()
            state["own"] = copy

        def spread_on():
            state["g2"] = []
            for way in range(2):
                state["g1"][way].wait_recv()
                start = t * width + step(x, 1 - way, NX) * part + way * half
                held = src_ref.at[core, :, :, :, pl.ds(pl.multiple_of(start, half), half)]
                state["g2"].append(send(held, held, g_send.at[t, 2 + way], g_recv.at[t, 2 + way],
                                        device(x_to=step(x, way, NX))))

        def twin():
            for copy in state["g2"]:
                copy.wait_recv()
            state["own"].wait()
            whole = src_ref.at[core, :, :, :, lanes]
            state["twin"] = send(whole, whole, e_send.at[t], e_recv.at[t], sibling)

        def finish():
            state["ring"][1 - t % 2].wait_recv()
            state["on"].wait_recv()
            state["twin"].wait_recv()

        return [begin] + [hop_stage(hop) for hop in range(1, NZ // 2 + 1)] + [
            pick, receivers, blend, choose, receivers_on, spread, spread_on, twin, finish]

    pieces = [piece(t) for t in range(PIECES)]
    for slot in range(len(pieces[0]) + SKEW * (PIECES - 1)):
        for t in range(PIECES):
            if 0 <= slot - SKEW * t < len(pieces[t]):
                pieces[t][slot - SKEW * t]()
    for copy in locals_started:
        copy.wait()
    for copy in sent:
        copy.wait_send()


def gather(records, live_mask, block_ids):
    shard, total = records.shape
    width = total // PIECES
    part = width // NX
    half = part // 2
    turns = block_ids.shape[0]
    live = jnp.broadcast_to(live_mask[:, None].astype(records.dtype), (shard, LANES))
    ids = jnp.zeros((8, LANES), jnp.int32).at[:turns].set(block_ids)
    dma = pltpu.SemaphoreType.DMA
    vmem = pl.BlockSpec(memory_space=pltpu.VMEM)
    buffers = [
        (NC, NZ, shard, width),
        (2, NY, 2, shard, half),
        (2, 2, NY, 2, shard, half),
        (2, 2, NY, 2, shard, half),
        (6, NY, 2, shard, half),
        (NY, 2, shard, part),
        (2, NY, shard, part),
    ]
    counts = [(PIECES, 2, 4), (PIECES, NZ), (PIECES, 4), (PIECES, 3), (PIECES, 4), (PIECES,),
              (PIECES, 3), (NY - 1,)]
    rcv, src = pl.pallas_call(
        gather_kernel,
        name="gather",
        in_specs=[vmem] * 3,
        out_specs=[vmem] * 2,
        out_shape=[
            jax.ShapeDtypeStruct((ZL, NY, shard, total), records.dtype),
            jax.ShapeDtypeStruct((turns, 2, NY, shard, total), records.dtype),
        ],
        scratch_shapes=(
            [pltpu.VMEM(shape, records.dtype) for shape in buffers for _ in range(PIECES)]
            + [pltpu.VMEM((NY, 8, LANES), jnp.int32), pltpu.SMEM((NY, 8, LANES), jnp.int32)]
            + [dma(shape) for shape in counts for _ in range(2)]
            + [dma((1 + 2 * PIECES,))]
        ),
        compiler_params=pltpu.CompilerParams(
            collective_id=0, has_side_effects=True, vmem_limit_bytes=40 * 1024 * 1024),
    )(records, live, ids)
    return rcv.reshape(-1, total), src.reshape(-1, total)


def local(records, live_mask, offsets, block_ids):
    members = records.shape[0] * lax.axis_size("src")
    rcv, src = gather(records, live_mask, block_ids)
    first = block_ids[:, 0] * SB
    group = lax.axis_index("rcv")
    chans = jnp.concatenate([first, (group * members)[None].astype(jnp.int32)])
    return compute(offsets, chans, rcv, src)


def solution(mesh):
    in_specs = (P(("rcv", "src"), None), P(("rcv", "src")), P(), P(None, "src"))
    out_specs = P(None, None, "src", "rcv")
    return jax.shard_map(local, mesh=mesh, in_specs=in_specs, out_specs=out_specs, check_vma=False)
```

```python
import jax
import jax.numpy as jnp
import numpy as np
from jax import lax
from jax.experimental import pallas as pl
from jax.experimental.pallas import tpu as pltpu
from jax.sharding import PartitionSpec as P

L = 256
SB = 128
LAGS = 76
LAGP = 80
BINS = L // 2
LANES = 128
SPAN = L + LANES
STRIDE = 132
GROUP = 32
LAST = (8192 - SPAN) // LANES
ROWS = 36


def tables(win_count):
    sample_axis = np.arange(L, dtype=np.float32)
    bin_axis = np.arange(BINS, dtype=np.float32)
    two_pi = np.float32(2.0 * np.pi)
    phases = two_pi * sample_axis[:, None] * bin_axis[None, :] / np.float32(L)
    taper = np.float32(0.5) - np.float32(0.5) * np.cos(two_pi * sample_axis / np.float32(L))
    dft = np.concatenate([taper[:, None] * np.cos(phases), -taper[:, None] * np.sin(phases)], axis=1)
    dft = dft.astype(jnp.bfloat16).astype(np.float32)
    shifted = np.zeros((L, SPAN), np.float32)
    shifted[:, :L] = dft.T
    lag_axis = np.arange(LAGS, dtype=np.float32)
    weights = np.where(bin_axis == 0, 1.0, 2.0).astype(np.float32)
    lag = (
        weights[:, None]
        * np.cos(two_pi * bin_axis[:, None] * lag_axis[None, :] / np.float32(L))
        * np.float32(2.0 / (win_count * L))
    )
    lag_t = np.zeros((LAGP, BINS), np.float32)
    lag_t[:LAGS] = lag.T
    padded = np.zeros((2, L + 2 * LANES, BINS), np.float32)
    padded[:, LANES:LANES + L] = dft.reshape(L, 2, BINS).transpose(1, 0, 2)
    return shifted, padded, lag_t.astype(jnp.bfloat16)


def windows(begin, end, unroll, off_ref, dft_ref, load, wide):
    win_count = off_ref.shape[0]

    @pl.loop(begin, end, unroll=unroll)
    def _(w):
        first = off_ref[w]
        base = jnp.minimum(first // LANES, LAST)
        samples = load(pl.ds(base * LANES, SPAN))
        if dft_ref.shape[0] == L:
            table = pltpu.roll(dft_ref[...], first - base * LANES, 1).astype(jnp.bfloat16)
            value = lax.dot_general(table, samples, (((1,), (1,)), ((), ())),
                                    preferred_element_type=jnp.float32)
            values = [value[part * BINS:(part + 1) * BINS] for part in range(2)]
        else:
            tables_t = [dft_ref[part, pl.ds(LANES - first + base * LANES, SPAN), :].astype(jnp.bfloat16)
                        for part in range(2)]
            values = [lax.dot_general(table, samples, (((0,), (1,)), ((), ())),
                                      preferred_element_type=jnp.float32) for table in tables_t]
        for half in range(2):
            for part in range(2):
                wide[half, pl.ds(part * win_count + w, BINS, stride=STRIDE), :] = (
                    values[part][:, half * LANES:(half + 1) * LANES])


def narrow(begin, end, taps, wide, store):
    @pl.loop(begin, end, unroll=8)
    def _(f):
        for half in range(2):
            rows = wide[half, pl.ds(pl.multiple_of(f * STRIDE, 4), taps), :]
            store(f, half, rows.astype(jnp.bfloat16))


def compute_kernel(off_ref, ids_ref, dft_ref, lag_ref, spec_ref, src_ref, out_ref,
                   spec_rcv, spec_src, wide, lagged, spec_sem):
    turn, group = pl.program_id(0), pl.program_id(1)
    win_count = off_ref.shape[0]
    taps = 2 * win_count
    rcv_first = lax.axis_index("rcv") * spec_rcv.shape[2]
    fetch = pltpu.make_async_copy(spec_ref, spec_rcv, spec_sem)

    @pl.when((turn == 0) & (group == 0))
    def _():
        fetch.start()

        def to_src(f, half, rows):
            spec_src[half, f] = rows

        windows(0, win_count, 8, off_ref, dft_ref, lambda span: src_ref[:, span], wide)
        narrow(0, BINS, taps, wide, to_src)
        fetch.wait()

    @pl.when(group == 0)
    def _():
        @pl.loop(0, BINS, unroll=8)
        def _(f):
            value = lax.dot_general(spec_src[turn, f], spec_rcv[f], (((0,), (0,)), ((), ())),
                                    preferred_element_type=jnp.float32)
            for half in range(2):
                wide[half, pl.ds(f, SB, stride=STRIDE), :] = value[:, half * LANES:(half + 1) * LANES]

    for s in range(GROUP):
        begin = pl.multiple_of((group * GROUP + s) * STRIDE, 4)
        cross = jnp.concatenate(
            [wide[half, pl.ds(begin, BINS), :].astype(jnp.bfloat16) for half in range(2)], axis=1)
        value = jnp.dot(lag_ref[...], cross, preferred_element_type=jnp.float32)
        for half in range(2):
            lagged[half, pl.ds(s, LAGP, stride=ROWS), :] = value[:, half * LANES:(half + 1) * LANES]
    src_chan = ids_ref[turn] * SB + group * GROUP + lax.broadcasted_iota(jnp.int32, (GROUP, LANES), 0)
    for half in range(2):
        rcv_chan = rcv_first + half * LANES + lax.broadcasted_iota(jnp.int32, (GROUP, LANES), 1)
        apart = src_chan != rcv_chan
        for lag in range(LAGS):
            value = lagged[half, lag * ROWS:lag * ROWS + GROUP, :]
            out_ref[0, lag, :, half * LANES:(half + 1) * LANES] = (
                jnp.where(apart, value, 0.0).astype(jnp.bfloat16))


def compute(offsets, block_ids, dft, lag, spec, src):
    win_count = offsets.shape[0]
    turns = block_ids.shape[0]
    bins, taps, rcv_total = spec.shape
    whole = lambda shape: pl.BlockSpec(shape, lambda t, g, *_: (0,) * len(shape), pipeline_mode=pl.Buffered(1))
    return pl.pallas_call(
        compute_kernel,
        name="correlate",
        grid_spec=pltpu.PrefetchScalarGridSpec(
            num_scalar_prefetch=2,
            grid=(turns, SB // GROUP),
            in_specs=[whole(dft.shape), whole(lag.shape), pl.BlockSpec(memory_space=pl.ANY), whole(src.shape)],
            out_specs=pl.BlockSpec((1, LAGS, GROUP, rcv_total), lambda t, g, *_: (t, 0, g, 0)),
            scratch_shapes=[
                pltpu.VMEM((bins, taps, rcv_total), jnp.bfloat16),
                pltpu.VMEM((turns, bins, taps, SB), jnp.bfloat16),
                pltpu.VMEM((2, BINS * STRIDE, LANES), jnp.float32),
                pltpu.VMEM((2, LAGP * ROWS, LANES), jnp.float32),
                pltpu.SemaphoreType.DMA,
            ],
        ),
        out_shape=jax.ShapeDtypeStruct((turns, LAGS, SB, rcv_total), jnp.bfloat16),
        compiler_params=pltpu.CompilerParams(vmem_limit_bytes=56 * 1024 * 1024),
    )(offsets, block_ids, dft, lag, spec, src)


NX, NY, NZ, NC = 4, 4, 8, 2
ZL = NZ // 2
PIECES = 4
OFFSETS = (0, 0, 0, 0)
MESH = pl.DeviceIdType.MESH


def gather_kernel(off_ref, live_ref, ids_ref, dft_ref, rec_ref, spec_out, src_out, rcv_ref, src_ref, spec_ref,
                  wide, *scratch):
    columns, first, mixed, second, landed, chosen, merged = (
        scratch[i * PIECES:(i + 1) * PIECES] for i in range(7))
    (id_buf, id_smem, z_send, z_recv, c_send, c_recv, x_send, x_recv, y_send, y_recv,
     g_send, g_recv, e_send, e_recv, r_send, r_recv, i_send, i_recv,
     local_sem) = scratch[7 * PIECES:]
    shard, total = rec_ref.shape
    width = total // PIECES
    part = width // NX
    half = part // 2

    src, rcv = lax.axis_index("src"), lax.axis_index("rcv")
    y, zl = src % NY, src // NY
    core, x, zh = rcv % NC, (rcv // NC) % NX, rcv // (NC * NX)
    z = zh * ZL + zl

    def device(x_to=x, y_to=y, z_to=z, core_to=core):
        return {"src": (z_to % ZL) * NY + y_to,
                "rcv": ((z_to // ZL) * NX + x_to) * NC + core_to}

    sent = []

    def send(src_ref, dst_ref, send_sem, recv_sem, to):
        copy = pltpu.make_async_remote_copy(
            src_ref=src_ref, dst_ref=dst_ref, send_sem=send_sem, recv_sem=recv_sem,
            device_id=to, device_id_type=MESH)
        copy.start()
        sent.append(copy)
        return copy

    def step(position, way, count):
        return (position + 1) % count if way == 0 else (position + count - 1) % count

    sibling = device(core_to=1 - core)
    barrier = pltpu.get_barrier_semaphore()
    peers = [device(z_to=step(z, way, NZ)) for way in range(2)] + [sibling]
    peers += [device(x_to=step(x, way, NX)) for way in range(2)]
    peers += [device(y_to=(y + d) % NY) for d in range(1, NY)]
    for peer in peers:
        pl.semaphore_signal(barrier, inc=1, device_id=peer, device_id_type=MESH)

    rows = lax.broadcasted_iota(jnp.int32, (shard, LANES), 0)
    live = jnp.zeros((shard, LANES), jnp.float32)
    for channel in range(shard):
        live = jnp.where(rows == channel, live_ref[channel].astype(jnp.float32), live)
    live = live[:, :1].astype(rec_ref.dtype)
    for t in range(PIECES):
        columns[t][core, z] = rec_ref[:, t * width:(t + 1) * width] * live
    id_buf[y] = jnp.where(lax.broadcasted_iota(jnp.int32, (8, LANES), 0) == 0, ids_ref[0], ids_ref[1])
    pl.semaphore_wait(barrier, len(peers))

    ids = [send(id_buf.at[y], id_buf.at[y], i_send.at[d - 1], i_recv.at[d - 1],
                device(y_to=(y + d) % NY)) for d in range(1, NY)]

    def ids_ready():
        for copy in ids:
            copy.wait_recv()
        to_smem = pltpu.make_async_copy(id_buf, id_smem, local_sem.at[0])
        to_smem.start()
        to_smem.wait()

    def piece(t):
        hops = (4, 3) if t % 2 == 0 else (3, 4)
        lanes = pl.ds(t * width, width)
        flying, shared = {}, []
        state = {}

        def hop_send(way, hop):
            slot = (z - (hop - 1) + NZ) % NZ if way == 0 else (z + (hop - 1)) % NZ
            flying[way] = send(columns[t].at[core, slot], columns[t].at[core, slot],
                               z_send.at[t, way, hop - 1], z_recv.at[t, way, hop - 1],
                               device(z_to=step(z, way, NZ)))

        def share(slot, index):
            shared.append(send(columns[t].at[core, slot], columns[t].at[core, slot],
                               c_send.at[t, index], c_recv.at[t, index], sibling))

        def begin():
            for way in range(2):
                hop_send(way, 1)
            share(z, 0)
            receivers(zl)

        def hop_stage(hop):
            def run():
                for way in range(2):
                    if hop <= hops[way]:
                        flying[way].wait_recv()
                        if hop < hops[way]:
                            hop_send(way, hop + 1)
                        share((z - hop + NZ) % NZ if way == 0 else (z + hop) % NZ, hop + way * hops[0])
                if hop < ZL:
                    receivers(jnp.where(zl == ZL - 1, ZL - 1 - hop, (zl + hop) % ZL))
            return run

        def ring_copy(way, src_ref, dst_ref):
            return pltpu.make_async_remote_copy(
                src_ref=src_ref, dst_ref=dst_ref, send_sem=r_send.at[t, way], recv_sem=r_recv.at[t, way],
                device_id=device(y_to=step(y, way, NY)), device_id_type=MESH)

        def receivers(member):
            own, target = columns[t].at[core, zh * ZL + member], rcv_ref.at[member, y, :, lanes]
            for way in range(2):
                ring_copy(way, own, target).start()
            pltpu.make_async_copy(own, target, local_sem.at[1 + t]).start()

        def ring_whole(way):
            return ring_copy(way, columns[t].at[core, pl.ds(zh * ZL, ZL)], rcv_ref.at[:, y, :, lanes])

        def receivers_on():
            way = t % 2
            ring_whole(way).wait_recv()
            held = rcv_ref.at[:, step(y, 1 - way, NY), :, lanes]
            state["on"] = send(held, held, r_send.at[t, 2], r_recv.at[t, 2], device(y_to=step(y, way, NY)))

        def pick():
            if t == 0:
                ids_ready()
            for copy in shared:
                copy.wait_recv()

            for y_of in range(NY):
                block = id_smem[y_of, core, 0]
                group = block // 2
                slot = (group // (NC * NX)) * ZL + (block % 2) * 2
                for p in range(2):
                    def take(q, h):
                        start = pl.multiple_of(q * part + h * half, half)
                        return columns[t][group % NC, slot + p, :, pl.ds(start, half)]

                    for h in range(2):
                        first[t][h, y_of, p] = take((x + 2) % NX, h)
                        landed[t][4 + h, y_of, p] = take(x, h)
                        mixed[t][h, 0, y_of, p] = take(step(x, h, NX), h)
                        second[t][h, 1, y_of, p] = take(step(x, h, NX), 1 - h)
            state["x1"] = [send(first[t].at[way], mixed[t].at[way, 1], x_send.at[t, way], x_recv.at[t, way],
                                device(x_to=step(x, way, NX))) for way in range(2)]

        def blend():
            for copy in state["x1"]:
                copy.wait_recv()
            state["x2"] = []
            for way in range(2):
                for y_of in range(NY):
                    root = (id_smem[y_of, core, 0] // (2 * NC)) % NX
                    other = jnp.where(root == step(x, 1 - way, NX), 1, 0)
                    second[t][way, 0, y_of] = mixed[t][way, other, y_of]
                state["x2"].append(send(second[t].at[way], landed[t].at[pl.ds(2 * way, 2)],
                                        x_send.at[t, 2 + way], x_recv.at[t, 2 + way],
                                        device(x_to=step(x, way, NX))))

        def choose():
            for copy in state["x2"]:
                copy.wait_recv()
            for y_of in range(NY):
                root = (id_smem[y_of, core, 0] // (2 * NC)) % NX
                away = (root - x + NX) % NX
                low = jnp.where(away == 0, 4, jnp.where(away == 1, 3, 0))
                high = jnp.where(away == 0, 5, jnp.where(away == 3, 1, 2))
                chosen[t][y_of, :, :, :half] = landed[t][low, y_of]
                chosen[t][y_of, :, :, half:] = landed[t][high, y_of]
            state["y"] = [send(chosen[t].at[(y + d) % NY], merged[t].at[:, y], y_send.at[t, d - 1],
                               y_recv.at[t, d - 1], device(y_to=(y + d) % NY)) for d in range(1, NY)]
            for p in range(2):
                merged[t][p, y] = chosen[t][y, p]

        def spread():
            for copy in state["y"]:
                copy.wait_recv()
            place = src_ref.at[core, :, :, :, pl.ds(t * width + x * part, part)]
            state["g1"] = [send(merged[t], place, g_send.at[t, way], g_recv.at[t, way],
                                device(x_to=step(x, way, NX))) for way in range(2)]
            copy = pltpu.make_async_copy(merged[t], place, local_sem.at[1 + PIECES + t])
            copy.start()
            state["own"] = copy

        def spread_on():
            state["g2"] = []
            for way in range(2):
                state["g1"][way].wait_recv()
                start = t * width + step(x, 1 - way, NX) * part + way * half
                held = src_ref.at[core, :, :, :, pl.ds(pl.multiple_of(start, half), half)]
                state["g2"].append(send(held, held, g_send.at[t, 2 + way], g_recv.at[t, 2 + way],
                                        device(x_to=step(x, way, NX))))

        def twin():
            for copy in state["g2"]:
                copy.wait_recv()
            state["own"].wait()
            whole = src_ref.at[core, :, :, :, lanes]
            state["twin"] = send(whole, whole, e_send.at[t], e_recv.at[t], sibling)

        def receivers_done():
            ring_whole(1 - t % 2).wait_recv()
            state["on"].wait_recv()
            for way in range(2):
                ring_whole(way).wait_send()
            pltpu.make_async_copy(columns[t].at[core, pl.ds(zh * ZL, ZL)], rcv_ref.at[:, y, :, lanes],
                                  local_sem.at[1 + t]).wait()

        def finish():
            state["twin"].wait_recv()
            held = src_ref.at[:, :, :, :, lanes]
            state["out"] = pltpu.make_async_copy(held, src_out.at[:, :, :, :, lanes], local_sem.at[1 + 2 * PIECES + t])
            state["out"].start()

        def end():
            state["out"].wait()

        return [begin] + [hop_stage(hop) for hop in range(1, NZ // 2 + 1)] + [
            pick, blend, receivers_on, choose, receivers_done, spread, spread_on, twin, finish, end]

    taps, count = spec_ref.shape[1], off_ref.shape[0]
    stored = []

    def to_spec(f, lane_half, values):
        spec_ref[f, :, lane_half * LANES:(lane_half + 1) * LANES] = values

    def windows_part(k, parts):
        windows(k * count // parts, (k + 1) * count // parts, 4, off_ref, dft_ref,
                lambda span: rcv_ref[:, :, :, span].reshape(ZL * NY * shard, SPAN), wide)

    def narrow_part(k, parts):
        size = BINS // parts
        narrow(k * size, (k + 1) * size, taps, wide, to_spec)
        piece_of = pl.ds(k * size, size)
        copy = pltpu.make_async_copy(spec_ref.at[piece_of], spec_out.at[piece_of],
                                     local_sem.at[1 + 3 * PIECES + k])
        copy.start()
        stored.append(copy)

    stages = [piece(t) for t in range(PIECES)]
    for slot in range(len(stages[0])):
        for t in range(PIECES):
            stages[t][slot]()
            late = slot - (len(stages[0]) - 5)
            if late in (0, 1):
                windows_part(late * PIECES + t, 2 * PIECES)
            if late == 2:
                narrow_part(t, PIECES)
    for copy in stored:
        copy.wait()
    for copy in sent:
        copy.wait_send()


def gather(records, live_mask, offsets, block_ids, dft):
    shard, total = records.shape
    width = total // PIECES
    part = width // NX
    half = part // 2
    turns = block_ids.shape[0]
    taps = 2 * offsets.shape[0]
    rcv_total = ZL * NY * shard
    dma = pltpu.SemaphoreType.DMA
    vmem = pl.BlockSpec(memory_space=pltpu.VMEM)
    smem = pl.BlockSpec(memory_space=pltpu.SMEM)
    hbm = pl.BlockSpec(memory_space=pl.ANY)
    buffers = [
        (NC, NZ, shard, width),
        (2, NY, 2, shard, half),
        (2, 2, NY, 2, shard, half),
        (2, 2, NY, 2, shard, half),
        (6, NY, 2, shard, half),
        (NY, 2, shard, part),
        (2, NY, shard, part),
    ]
    counts = [(PIECES, 2, 4), (PIECES, NZ), (PIECES, 4), (PIECES, 3), (PIECES, 4), (PIECES,),
              (PIECES, 3), (NY - 1,)]
    src_shape = (turns, 2, NY, shard, total)
    spec, src = pl.pallas_call(
        gather_kernel,
        name="gather",
        in_specs=[smem] * 3 + [vmem] * 2,
        out_specs=[hbm] * 2,
        out_shape=[
            jax.ShapeDtypeStruct((BINS, taps, rcv_total), records.dtype),
            jax.ShapeDtypeStruct(src_shape, records.dtype),
        ],
        scratch_shapes=(
            [
                pltpu.VMEM((ZL, NY, shard, total), records.dtype),
                pltpu.VMEM(src_shape, records.dtype),
                pltpu.VMEM((BINS, taps, rcv_total), records.dtype),
                pltpu.VMEM((2, BINS * STRIDE, LANES), jnp.float32),
            ]
            + [pltpu.VMEM(shape, records.dtype) for shape in buffers for _ in range(PIECES)]
            + [pltpu.VMEM((NY, 8, LANES), jnp.int32), pltpu.SMEM((NY, 8, LANES), jnp.int32)]
            + [dma(shape) for shape in counts for _ in range(2)]
            + [dma((1 + 4 * PIECES,))]
        ),
        compiler_params=pltpu.CompilerParams(
            collective_id=0, has_side_effects=True, vmem_limit_bytes=56 * 1024 * 1024),
    )(offsets, live_mask, block_ids, dft, records)
    return spec, src.reshape(-1, total)


def local(records, live_mask, offsets, block_ids):
    dft, padded, lag = tables(offsets.shape[0])
    block_ids = block_ids.reshape(-1)
    spec, src = gather(records, live_mask, offsets, block_ids, padded)
    return compute(offsets, block_ids, dft, lag, spec, src)


def solution(mesh):
    in_specs = (P(("rcv", "src"), None), P(("rcv", "src")), P(), P(None, "src"))
    out_specs = P(None, None, "src", "rcv")
    return jax.shard_map(local, mesh=mesh, in_specs=in_specs, out_specs=out_specs, check_vma=False)
```

```python
import jax
import jax.numpy as jnp
import numpy as np
from jax import lax
from jax.experimental import pallas as pl
from jax.experimental.pallas import tpu as pltpu
from jax.sharding import PartitionSpec as P

L = 256
SB = 128
LAGS = 76
LAGP = 80
BINS = L // 2
LANES = 128
SPAN = L + LANES
STRIDE = 132
GROUP = 32
LAST = (8192 - SPAN) // LANES
ROWS = 36


def tables(win_count):
    sample_axis = np.arange(L, dtype=np.float32)
    bin_axis = np.arange(BINS, dtype=np.float32)
    two_pi = np.float32(2.0 * np.pi)
    phases = two_pi * sample_axis[:, None] * bin_axis[None, :] / np.float32(L)
    taper = np.float32(0.5) - np.float32(0.5) * np.cos(two_pi * sample_axis / np.float32(L))
    dft = np.concatenate([taper[:, None] * np.cos(phases), -taper[:, None] * np.sin(phases)], axis=1)
    dft = dft.astype(jnp.bfloat16).astype(np.float32)
    shifted = np.zeros((L, SPAN), np.float32)
    shifted[:, :L] = dft.T
    lag_axis = np.arange(LAGS, dtype=np.float32)
    weights = np.where(bin_axis == 0, 1.0, 2.0).astype(np.float32)
    lag = (
        weights[:, None]
        * np.cos(two_pi * bin_axis[:, None] * lag_axis[None, :] / np.float32(L))
        * np.float32(2.0 / (win_count * L))
    )
    lag_t = np.zeros((LAGP, BINS), np.float32)
    lag_t[:LAGS] = lag.T
    padded = np.zeros((2, L + 2 * LANES, BINS), np.float32)
    padded[:, LANES:LANES + L] = dft.reshape(L, 2, BINS).transpose(1, 0, 2)
    return shifted, padded, lag_t.astype(jnp.bfloat16)


def windows(begin, end, unroll, off_ref, dft_ref, load, wide):
    win_count = off_ref.shape[0]

    @pl.loop(begin, end, unroll=unroll)
    def _(w):
        first = off_ref[w]
        base = jnp.minimum(first // LANES, LAST)
        samples = load(pl.ds(base * LANES, SPAN))
        if dft_ref.shape[0] == L:
            table = pltpu.roll(dft_ref[...], first - base * LANES, 1).astype(jnp.bfloat16)
            value = lax.dot_general(table, samples, (((1,), (1,)), ((), ())),
                                    preferred_element_type=jnp.float32)
            values = [value[part * BINS:(part + 1) * BINS] for part in range(2)]
        else:
            tables_t = [dft_ref[part, pl.ds(LANES - first + base * LANES, SPAN), :].astype(jnp.bfloat16)
                        for part in range(2)]
            values = [lax.dot_general(table, samples, (((0,), (1,)), ((), ())),
                                      preferred_element_type=jnp.float32) for table in tables_t]
        for half in range(2):
            for part in range(2):
                wide[half, pl.ds(part * win_count + w, BINS, stride=STRIDE), :] = (
                    values[part][:, half * LANES:(half + 1) * LANES])


def narrow(begin, end, taps, wide, store):
    @pl.loop(begin, end, unroll=8)
    def _(f):
        for half in range(2):
            rows = wide[half, pl.ds(pl.multiple_of(f * STRIDE, 4), taps), :]
            store(f, half, rows.astype(jnp.bfloat16))


def compute_kernel(off_ref, ids_ref, dft_ref, lag_ref, spec_ref, src_ref, out_ref,
                   spec_rcv, spec_src, wide, lagged, spec_sem):
    turn, group = pl.program_id(0), pl.program_id(1)
    win_count = off_ref.shape[0]
    taps = 2 * win_count
    rcv_first = lax.axis_index("rcv") * spec_rcv.shape[2]
    fetch = pltpu.make_async_copy(spec_ref, spec_rcv, spec_sem)

    @pl.when((turn == 0) & (group == 0))
    def _():
        fetch.start()

        windows(0, win_count, 8, off_ref, dft_ref, lambda span: src_ref[:, span], spec_src)
        fetch.wait()

    @pl.when(group == 0)
    def _():
        @pl.loop(0, BINS, unroll=8)
        def _(f):
            source = spec_src[turn, pl.ds(pl.multiple_of(f * STRIDE, 4), taps), :].astype(jnp.bfloat16)
            value = lax.dot_general(source, spec_rcv[f], (((0,), (0,)), ((), ())),
                                    preferred_element_type=jnp.float32)
            for half in range(2):
                wide[half, pl.ds(f, SB, stride=STRIDE), :] = value[:, half * LANES:(half + 1) * LANES]

    for s in range(GROUP):
        begin = pl.multiple_of((group * GROUP + s) * STRIDE, 4)
        cross = jnp.concatenate(
            [wide[half, pl.ds(begin, BINS), :].astype(jnp.bfloat16) for half in range(2)], axis=1)
        value = jnp.dot(lag_ref[...], cross, preferred_element_type=jnp.float32)
        for half in range(2):
            lagged[half, pl.ds(s, LAGP, stride=ROWS), :] = value[:, half * LANES:(half + 1) * LANES]
    src_chan = ids_ref[turn] * SB + group * GROUP + lax.broadcasted_iota(jnp.int32, (GROUP, LANES), 0)
    for half in range(2):
        rcv_chan = rcv_first + half * LANES + lax.broadcasted_iota(jnp.int32, (GROUP, LANES), 1)
        apart = src_chan != rcv_chan
        for lag in range(LAGS):
            value = lagged[half, lag * ROWS:lag * ROWS + GROUP, :]
            out_ref[0, lag, :, half * LANES:(half + 1) * LANES] = (
                jnp.where(apart, value, 0.0).astype(jnp.bfloat16))


def compute(offsets, block_ids, dft, lag, spec, src):
    win_count = offsets.shape[0]
    turns = block_ids.shape[0]
    bins, taps, rcv_total = spec.shape
    whole = lambda shape: pl.BlockSpec(shape, lambda t, g, *_: (0,) * len(shape), pipeline_mode=pl.Buffered(1))
    return pl.pallas_call(
        compute_kernel,
        name="correlate",
        grid_spec=pltpu.PrefetchScalarGridSpec(
            num_scalar_prefetch=2,
            grid=(turns, SB // GROUP),
            in_specs=[whole(dft.shape), whole(lag.shape), pl.BlockSpec(memory_space=pl.ANY), whole(src.shape)],
            out_specs=pl.BlockSpec((1, LAGS, GROUP, rcv_total), lambda t, g, *_: (t, 0, g, 0)),
            scratch_shapes=[
                pltpu.VMEM((bins, taps, rcv_total), jnp.bfloat16),
                pltpu.VMEM((turns, BINS * STRIDE, SB), jnp.float32),
                pltpu.VMEM((2, BINS * STRIDE, LANES), jnp.float32),
                pltpu.VMEM((2, LAGP * ROWS, LANES), jnp.float32),
                pltpu.SemaphoreType.DMA,
            ],
        ),
        out_shape=jax.ShapeDtypeStruct((turns, LAGS, SB, rcv_total), jnp.bfloat16),
        compiler_params=pltpu.CompilerParams(vmem_limit_bytes=60 * 1024 * 1024),
    )(offsets, block_ids, dft, lag, spec, src)


NX, NY, NZ, NC = 4, 4, 8, 2
ZL = NZ // 2
PIECES = 4
OFFSETS = (0, 0, 0, 0)
MESH = pl.DeviceIdType.MESH


def gather_kernel(off_ref, live_ref, ids_ref, dft_ref, rec_ref, spec_out, src_out, rcv_ref, src_ref, spec_ref,
                  wide, *scratch):
    columns, first, mixed, second, landed, chosen, merged = (
        scratch[i * PIECES:(i + 1) * PIECES] for i in range(7))
    (id_buf, id_smem, z_send, z_recv, c_send, c_recv, x_send, x_recv, y_send, y_recv,
     g_send, g_recv, e_send, e_recv, r_send, r_recv, i_send, i_recv,
     local_sem) = scratch[7 * PIECES:]
    shard, total = rec_ref.shape
    width = total // PIECES
    part = width // NX
    half = part // 2

    src, rcv = lax.axis_index("src"), lax.axis_index("rcv")
    y, zl = src % NY, src // NY
    core, x, zh = rcv % NC, (rcv // NC) % NX, rcv // (NC * NX)
    z = zh * ZL + zl

    def device(x_to=x, y_to=y, z_to=z, core_to=core):
        return {"src": (z_to % ZL) * NY + y_to,
                "rcv": ((z_to // ZL) * NX + x_to) * NC + core_to}

    sent = []

    def send(src_ref, dst_ref, send_sem, recv_sem, to):
        copy = pltpu.make_async_remote_copy(
            src_ref=src_ref, dst_ref=dst_ref, send_sem=send_sem, recv_sem=recv_sem,
            device_id=to, device_id_type=MESH)
        copy.start()
        sent.append(copy)
        return copy

    def step(position, way, count):
        return (position + 1) % count if way == 0 else (position + count - 1) % count

    sibling = device(core_to=1 - core)
    barrier = pltpu.get_barrier_semaphore()
    peers = [device(z_to=step(z, way, NZ)) for way in range(2)] + [sibling]
    peers += [device(x_to=step(x, way, NX)) for way in range(2)]
    peers += [device(y_to=(y + d) % NY) for d in range(1, NY)]
    for peer in peers:
        pl.semaphore_signal(barrier, inc=1, device_id=peer, device_id_type=MESH)

    rows = lax.broadcasted_iota(jnp.int32, (shard, LANES), 0)
    live = jnp.zeros((shard, LANES), jnp.float32)
    for channel in range(shard):
        live = jnp.where(rows == channel, live_ref[channel].astype(jnp.float32), live)
    live = live[:, :1].astype(rec_ref.dtype)
    for t in range(PIECES):
        columns[t][core, z] = rec_ref[:, t * width:(t + 1) * width] * live
    id_buf[y] = jnp.where(lax.broadcasted_iota(jnp.int32, (8, LANES), 0) == 0, ids_ref[0], ids_ref[1])
    pl.semaphore_wait(barrier, len(peers))

    ids = [send(id_buf.at[y], id_buf.at[y], i_send.at[d - 1], i_recv.at[d - 1],
                device(y_to=(y + d) % NY)) for d in range(1, NY)]

    def ids_ready():
        for copy in ids:
            copy.wait_recv()
        to_smem = pltpu.make_async_copy(id_buf, id_smem, local_sem.at[0])
        to_smem.start()
        to_smem.wait()

    def piece(t):
        hops = (4, 3) if t % 2 == 0 else (3, 4)
        lanes = pl.ds(t * width, width)
        flying, shared = {}, []
        state = {}

        def hop_send(way, hop):
            slot = (z - (hop - 1) + NZ) % NZ if way == 0 else (z + (hop - 1)) % NZ
            flying[way] = send(columns[t].at[core, slot], columns[t].at[core, slot],
                               z_send.at[t, way, hop - 1], z_recv.at[t, way, hop - 1],
                               device(z_to=step(z, way, NZ)))

        def share(slot, index):
            shared.append(send(columns[t].at[core, slot], columns[t].at[core, slot],
                               c_send.at[t, index], c_recv.at[t, index], sibling))

        def begin():
            for way in range(2):
                hop_send(way, 1)
            share(z, 0)
            receivers(zl)

        def hop_stage(hop):
            def run():
                for way in range(2):
                    if hop <= hops[way]:
                        flying[way].wait_recv()
                        if hop < hops[way]:
                            hop_send(way, hop + 1)
                        share((z - hop + NZ) % NZ if way == 0 else (z + hop) % NZ, hop + way * hops[0])
                if hop < ZL:
                    receivers(jnp.where(zl == ZL - 1, ZL - 1 - hop, (zl + hop) % ZL))
            return run

        def ring_copy(way, src_ref, dst_ref):
            return pltpu.make_async_remote_copy(
                src_ref=src_ref, dst_ref=dst_ref, send_sem=r_send.at[t, way], recv_sem=r_recv.at[t, way],
                device_id=device(y_to=step(y, way, NY)), device_id_type=MESH)

        def receivers(member):
            own, target = columns[t].at[core, zh * ZL + member], rcv_ref.at[member, y, :, lanes]
            for way in range(2):
                ring_copy(way, own, target).start()
            pltpu.make_async_copy(own, target, local_sem.at[1 + t]).start()

        def ring_whole(way):
            return ring_copy(way, columns[t].at[core, pl.ds(zh * ZL, ZL)], rcv_ref.at[:, y, :, lanes])

        def receivers_on():
            way = t % 2
            ring_whole(way).wait_recv()
            held = rcv_ref.at[:, step(y, 1 - way, NY), :, lanes]
            state["on"] = send(held, held, r_send.at[t, 2], r_recv.at[t, 2], device(y_to=step(y, way, NY)))

        def pick():
            if t == 0:
                ids_ready()
            for copy in shared:
                copy.wait_recv()

            for y_of in range(NY):
                block = id_smem[y_of, core, 0]
                group = block // 2
                slot = (group // (NC * NX)) * ZL + (block % 2) * 2
                for p in range(2):
                    def take(q, h):
                        start = pl.multiple_of(q * part + h * half, half)
                        return columns[t][group % NC, slot + p, :, pl.ds(start, half)]

                    for h in range(2):
                        first[t][h, y_of, p] = take((x + 2) % NX, h)
                        landed[t][4 + h, y_of, p] = take(x, h)
                        mixed[t][h, 0, y_of, p] = take(step(x, h, NX), h)
                        second[t][h, 1, y_of, p] = take(step(x, h, NX), 1 - h)
            state["x1"] = [send(first[t].at[way], mixed[t].at[way, 1], x_send.at[t, way], x_recv.at[t, way],
                                device(x_to=step(x, way, NX))) for way in range(2)]

        def blend():
            for copy in state["x1"]:
                copy.wait_recv()
            state["x2"] = []
            for way in range(2):
                for y_of in range(NY):
                    root = (id_smem[y_of, core, 0] // (2 * NC)) % NX
                    other = jnp.where(root == step(x, 1 - way, NX), 1, 0)
                    second[t][way, 0, y_of] = mixed[t][way, other, y_of]
                state["x2"].append(send(second[t].at[way], landed[t].at[pl.ds(2 * way, 2)],
                                        x_send.at[t, 2 + way], x_recv.at[t, 2 + way],
                                        device(x_to=step(x, way, NX))))

        def choose():
            for copy in state["x2"]:
                copy.wait_recv()
            for y_of in range(NY):
                root = (id_smem[y_of, core, 0] // (2 * NC)) % NX
                away = (root - x + NX) % NX
                low = jnp.where(away == 0, 4, jnp.where(away == 1, 3, 0))
                high = jnp.where(away == 0, 5, jnp.where(away == 3, 1, 2))
                chosen[t][y_of, :, :, :half] = landed[t][low, y_of]
                chosen[t][y_of, :, :, half:] = landed[t][high, y_of]
            state["y"] = [send(chosen[t].at[(y + d) % NY], merged[t].at[:, y], y_send.at[t, d - 1],
                               y_recv.at[t, d - 1], device(y_to=(y + d) % NY)) for d in range(1, NY)]
            for p in range(2):
                merged[t][p, y] = chosen[t][y, p]

        def spread():
            for copy in state["y"]:
                copy.wait_recv()
            place = src_ref.at[core, :, :, :, pl.ds(t * width + x * part, part)]
            state["g1"] = [send(merged[t], place, g_send.at[t, way], g_recv.at[t, way],
                                device(x_to=step(x, way, NX))) for way in range(2)]
            copy = pltpu.make_async_copy(merged[t], place, local_sem.at[1 + PIECES + t])
            copy.start()
            state["own"] = copy

        def spread_on():
            state["g2"] = []
            for way in range(2):
                state["g1"][way].wait_recv()
                start = t * width + step(x, 1 - way, NX) * part + way * half
                held = src_ref.at[core, :, :, :, pl.ds(pl.multiple_of(start, half), half)]
                state["g2"].append(send(held, held, g_send.at[t, 2 + way], g_recv.at[t, 2 + way],
                                        device(x_to=step(x, way, NX))))

        def twin():
            for copy in state["g2"]:
                copy.wait_recv()
            state["own"].wait()
            whole = src_ref.at[core, :, :, :, lanes]
            state["twin"] = send(whole, whole, e_send.at[t], e_recv.at[t], sibling)

        def receivers_done():
            ring_whole(1 - t % 2).wait_recv()
            state["on"].wait_recv()
            for way in range(2):
                ring_whole(way).wait_send()
            pltpu.make_async_copy(columns[t].at[core, pl.ds(zh * ZL, ZL)], rcv_ref.at[:, y, :, lanes],
                                  local_sem.at[1 + t]).wait()

        def finish():
            state["twin"].wait_recv()
            held = src_ref.at[:, :, :, :, lanes]
            state["out"] = pltpu.make_async_copy(held, src_out.at[:, :, :, :, lanes], local_sem.at[1 + 2 * PIECES + t])
            state["out"].start()

        def end():
            state["out"].wait()

        return [begin] + [hop_stage(hop) for hop in range(1, NZ // 2 + 1)] + [
            pick, receivers_on, blend, choose, receivers_done, spread, spread_on, twin, finish, end]

    taps, count = spec_ref.shape[1], off_ref.shape[0]
    stored = []

    def to_spec(f, lane_half, values):
        spec_ref[f, :, lane_half * LANES:(lane_half + 1) * LANES] = values

    def windows_part(k, parts):
        windows(k * count // parts, (k + 1) * count // parts, 4, off_ref, dft_ref,
                lambda span: rcv_ref[:, :, :, span].reshape(ZL * NY * shard, SPAN), wide)

    def narrow_part(k, parts):
        size = BINS // parts
        narrow(k * size, (k + 1) * size, taps, wide, to_spec)
        piece_of = pl.ds(k * size, size)
        copy = pltpu.make_async_copy(spec_ref.at[piece_of], spec_out.at[piece_of],
                                     local_sem.at[1 + 3 * PIECES + k])
        copy.start()
        stored.append(copy)

    stages = [piece(t) for t in range(PIECES)]
    for slot in range(len(stages[0])):
        for t in range(PIECES):
            stages[t][slot]()
            late = slot - (len(stages[0]) - 5)
            if late in (0, 1):
                windows_part(late * PIECES + t, 2 * PIECES)
            if late == 2:
                narrow_part(t, PIECES)
    for copy in stored:
        copy.wait()
    for copy in sent:
        copy.wait_send()


def gather(records, live_mask, offsets, block_ids, dft):
    shard, total = records.shape
    width = total // PIECES
    part = width // NX
    half = part // 2
    turns = block_ids.shape[0]
    taps = 2 * offsets.shape[0]
    rcv_total = ZL * NY * shard
    dma = pltpu.SemaphoreType.DMA
    vmem = pl.BlockSpec(memory_space=pltpu.VMEM)
    smem = pl.BlockSpec(memory_space=pltpu.SMEM)
    hbm = pl.BlockSpec(memory_space=pl.ANY)
    buffers = [
        (NC, NZ, shard, width),
        (2, NY, 2, shard, half),
        (2, 2, NY, 2, shard, half),
        (2, 2, NY, 2, shard, half),
        (6, NY, 2, shard, half),
        (NY, 2, shard, part),
        (2, NY, shard, part),
    ]
    counts = [(PIECES, 2, 4), (PIECES, NZ), (PIECES, 4), (PIECES, 3), (PIECES, 4), (PIECES,),
              (PIECES, 3), (NY - 1,)]
    src_shape = (turns, 2, NY, shard, total)
    spec, src = pl.pallas_call(
        gather_kernel,
        name="gather",
        in_specs=[smem] * 3 + [vmem] * 2,
        out_specs=[hbm] * 2,
        out_shape=[
            jax.ShapeDtypeStruct((BINS, taps, rcv_total), records.dtype),
            jax.ShapeDtypeStruct(src_shape, records.dtype),
        ],
        scratch_shapes=(
            [
                pltpu.VMEM((ZL, NY, shard, total), records.dtype),
                pltpu.VMEM(src_shape, records.dtype),
                pltpu.VMEM((BINS, taps, rcv_total), records.dtype),
                pltpu.VMEM((2, BINS * STRIDE, LANES), jnp.float32),
            ]
            + [pltpu.VMEM(shape, records.dtype) for shape in buffers for _ in range(PIECES)]
            + [pltpu.VMEM((NY, 8, LANES), jnp.int32), pltpu.SMEM((NY, 8, LANES), jnp.int32)]
            + [dma(shape) for shape in counts for _ in range(2)]
            + [dma((1 + 4 * PIECES,))]
        ),
        compiler_params=pltpu.CompilerParams(
            collective_id=0, has_side_effects=True, vmem_limit_bytes=56 * 1024 * 1024),
    )(offsets, live_mask, block_ids, dft, records)
    return spec, src.reshape(-1, total)


def local(records, live_mask, offsets, block_ids):
    dft, padded, lag = tables(offsets.shape[0])
    block_ids = block_ids.reshape(-1)
    spec, src = gather(records, live_mask, offsets, block_ids, padded)
    return compute(offsets, block_ids, dft, lag, spec, src)


def solution(mesh):
    in_specs = (P(("rcv", "src"), None), P(("rcv", "src")), P(), P(None, "src"))
    out_specs = P(None, None, "src", "rcv")
    return jax.shard_map(local, mesh=mesh, in_specs=in_specs, out_specs=out_specs, check_vma=False)
```

```python
import jax
import jax.numpy as jnp
import numpy as np
from jax import lax
from jax.experimental import pallas as pl
from jax.experimental.pallas import tpu as pltpu
from jax.sharding import PartitionSpec as P

L = 256
SB = 128
LAGS = 76
LAGP = 80
BINS = L // 2
LANES = 128
SPAN = L + LANES
STRIDE = 132
GROUP = 64
LAST = (8192 - SPAN) // LANES
ROWS = 68


def tables(win_count):
    sample_axis = np.arange(L, dtype=np.float32)
    bin_axis = np.arange(BINS, dtype=np.float32)
    two_pi = np.float32(2.0 * np.pi)
    phases = two_pi * sample_axis[:, None] * bin_axis[None, :] / np.float32(L)
    taper = np.float32(0.5) - np.float32(0.5) * np.cos(two_pi * sample_axis / np.float32(L))
    dft = np.concatenate([taper[:, None] * np.cos(phases), -taper[:, None] * np.sin(phases)], axis=1)
    dft = dft.astype(jnp.bfloat16).astype(np.float32)
    shifted = np.zeros((L, SPAN), np.float32)
    shifted[:, :L] = dft.T
    lag_axis = np.arange(LAGS, dtype=np.float32)
    weights = np.where(bin_axis == 0, 1.0, 2.0).astype(np.float32)
    lag = (
        weights[:, None]
        * np.cos(two_pi * bin_axis[:, None] * lag_axis[None, :] / np.float32(L))
        * np.float32(2.0 / (win_count * L))
    )
    lag_t = np.zeros((LAGP, BINS), np.float32)
    lag_t[:LAGS] = lag.T
    padded = np.zeros((2, L + 2 * LANES, BINS), np.float32)
    padded[:, LANES:LANES + L] = dft.reshape(L, 2, BINS).transpose(1, 0, 2)
    return shifted, padded, lag_t.astype(jnp.bfloat16)


def windows(begin, end, unroll, off_ref, dft_ref, load, wide):
    win_count = off_ref.shape[0]

    @pl.loop(begin, end, unroll=unroll)
    def _(w):
        first = off_ref[w]
        base = jnp.minimum(first // LANES, LAST)
        samples = load(pl.ds(base * LANES, SPAN))
        if dft_ref.shape[0] == L:
            table = pltpu.roll(dft_ref[...], first - base * LANES, 1).astype(jnp.bfloat16)
            value = lax.dot_general(table, samples, (((1,), (1,)), ((), ())),
                                    preferred_element_type=jnp.float32)
            values = [value[part * BINS:(part + 1) * BINS] for part in range(2)]
        else:
            tables_t = [dft_ref[part, pl.ds(LANES - first + base * LANES, SPAN), :].astype(jnp.bfloat16)
                        for part in range(2)]
            values = [lax.dot_general(table, samples, (((0,), (1,)), ((), ())),
                                      preferred_element_type=jnp.float32) for table in tables_t]
        for half in range(2):
            for part in range(2):
                wide[half, pl.ds(part * win_count + w, BINS, stride=STRIDE), :] = (
                    values[part][:, half * LANES:(half + 1) * LANES])


def narrow(begin, end, taps, wide, store):
    @pl.loop(begin, end, unroll=8)
    def _(f):
        for half in range(2):
            rows = wide[half, pl.ds(pl.multiple_of(f * STRIDE, 4), taps), :]
            store(f, half, rows.astype(jnp.bfloat16))


def compute_kernel(off_ref, ids_ref, dft_ref, lag_ref, spec_ref, src_ref, out_ref,
                   spec_rcv, spec_src, wide, lagged, spec_sem):
    turn, group = pl.program_id(0), pl.program_id(1)
    win_count = off_ref.shape[0]
    taps = 2 * win_count
    rcv_first = lax.axis_index("rcv") * spec_rcv.shape[2]
    fetch = pltpu.make_async_copy(spec_ref, spec_rcv, spec_sem)

    @pl.when((turn == 0) & (group == 0))
    def _():
        fetch.start()

        windows(0, win_count, 16, off_ref, dft_ref, lambda span: src_ref[:, span], spec_src)
        fetch.wait()

    @pl.when(group == 0)
    def _():
        @pl.loop(0, BINS, unroll=32)
        def _(f):
            source = spec_src[turn, pl.ds(pl.multiple_of(f * STRIDE, 4), taps), :].astype(jnp.bfloat16)
            value = lax.dot_general(source, spec_rcv[f], (((0,), (0,)), ((), ())),
                                    preferred_element_type=jnp.float32)
            for half in range(2):
                wide[half, pl.ds(f, SB, stride=STRIDE), :] = value[:, half * LANES:(half + 1) * LANES]

    for s in range(GROUP):
        begin = pl.multiple_of((group * GROUP + s) * STRIDE, 4)
        cross = jnp.concatenate(
            [wide[half, pl.ds(begin, BINS), :].astype(jnp.bfloat16) for half in range(2)], axis=1)
        value = jnp.dot(lag_ref[...], cross, preferred_element_type=jnp.float32)
        for half in range(2):
            lagged[half, pl.ds(s, LAGP, stride=ROWS), :] = value[:, half * LANES:(half + 1) * LANES]
    src_chan = ids_ref[turn] * SB + group * GROUP + lax.broadcasted_iota(jnp.int32, (GROUP, LANES), 0)
    for half in range(2):
        rcv_chan = rcv_first + half * LANES + lax.broadcasted_iota(jnp.int32, (GROUP, LANES), 1)
        apart = src_chan != rcv_chan
        for lag in range(LAGS):
            value = lagged[half, lag * ROWS:lag * ROWS + GROUP, :]
            out_ref[0, lag, :, half * LANES:(half + 1) * LANES] = (
                jnp.where(apart, value, 0.0).astype(jnp.bfloat16))


def compute(offsets, block_ids, dft, lag, spec, src):
    win_count = offsets.shape[0]
    turns = block_ids.shape[0]
    bins, taps, rcv_total = spec.shape
    whole = lambda shape: pl.BlockSpec(shape, lambda t, g, *_: (0,) * len(shape), pipeline_mode=pl.Buffered(1))
    return pl.pallas_call(
        compute_kernel,
        name="correlate",
        grid_spec=pltpu.PrefetchScalarGridSpec(
            num_scalar_prefetch=2,
            grid=(turns, SB // GROUP),
            in_specs=[whole(dft.shape), whole(lag.shape), pl.BlockSpec(memory_space=pl.ANY), whole(src.shape)],
            out_specs=pl.BlockSpec((1, LAGS, GROUP, rcv_total), lambda t, g, *_: (t, 0, g, 0)),
            scratch_shapes=[
                pltpu.VMEM((bins, taps, rcv_total), jnp.bfloat16),
                pltpu.VMEM((turns, BINS * STRIDE, SB), jnp.float32),
                pltpu.VMEM((2, BINS * STRIDE, LANES), jnp.float32),
                pltpu.VMEM((2, LAGP * ROWS, LANES), jnp.float32),
                pltpu.SemaphoreType.DMA,
            ],
        ),
        out_shape=jax.ShapeDtypeStruct((turns, LAGS, SB, rcv_total), jnp.bfloat16),
        compiler_params=pltpu.CompilerParams(vmem_limit_bytes=60 * 1024 * 1024),
    )(offsets, block_ids, dft, lag, spec, src)


NX, NY, NZ, NC = 4, 4, 8, 2
ZL = NZ // 2
PIECES = 4
OFFSETS = (0, 0, 0, 0)
MESH = pl.DeviceIdType.MESH


def gather_kernel(off_ref, live_ref, ids_ref, dft_ref, rec_ref, spec_out, src_out, rcv_ref, src_ref, spec_ref,
                  wide, *scratch):
    columns, first, mixed, second, landed, chosen, merged = (
        scratch[i * PIECES:(i + 1) * PIECES] for i in range(7))
    (id_buf, id_smem, z_send, z_recv, c_send, c_recv, x_send, x_recv, y_send, y_recv,
     g_send, g_recv, e_send, e_recv, r_send, r_recv, i_send, i_recv,
     local_sem) = scratch[7 * PIECES:]
    shard, total = rec_ref.shape
    width = total // PIECES
    part = width // NX
    half = part // 2

    src, rcv = lax.axis_index("src"), lax.axis_index("rcv")
    y, zl = src % NY, src // NY
    core, x, zh = rcv % NC, (rcv // NC) % NX, rcv // (NC * NX)
    z = zh * ZL + zl

    def device(x_to=x, y_to=y, z_to=z, core_to=core):
        return {"src": (z_to % ZL) * NY + y_to,
                "rcv": ((z_to // ZL) * NX + x_to) * NC + core_to}

    sent = []

    def send(src_ref, dst_ref, send_sem, recv_sem, to):
        copy = pltpu.make_async_remote_copy(
            src_ref=src_ref, dst_ref=dst_ref, send_sem=send_sem, recv_sem=recv_sem,
            device_id=to, device_id_type=MESH)
        copy.start()
        sent.append(copy)
        return copy

    def step(position, way, count):
        return (position + 1) % count if way == 0 else (position + count - 1) % count

    sibling = device(core_to=1 - core)
    barrier = pltpu.get_barrier_semaphore()
    peers = [device(z_to=step(z, way, NZ)) for way in range(2)] + [sibling]
    peers += [device(x_to=step(x, way, NX)) for way in range(2)]
    peers += [device(y_to=(y + d) % NY) for d in range(1, NY)]
    for peer in peers:
        pl.semaphore_signal(barrier, inc=1, device_id=peer, device_id_type=MESH)

    rows = lax.broadcasted_iota(jnp.int32, (shard, LANES), 0)
    live = jnp.zeros((shard, LANES), jnp.float32)
    for channel in range(shard):
        live = jnp.where(rows == channel, live_ref[channel].astype(jnp.float32), live)
    live = live[:, :1].astype(rec_ref.dtype)
    for t in range(PIECES):
        columns[t][core, z] = rec_ref[:, t * width:(t + 1) * width] * live
    id_buf[y] = jnp.where(lax.broadcasted_iota(jnp.int32, (8, LANES), 0) == 0, ids_ref[0], ids_ref[1])
    pl.semaphore_wait(barrier, len(peers))

    ids = [send(id_buf.at[y], id_buf.at[y], i_send.at[d - 1], i_recv.at[d - 1],
                device(y_to=(y + d) % NY)) for d in range(1, NY)]

    def ids_ready():
        for copy in ids:
            copy.wait_recv()
        to_smem = pltpu.make_async_copy(id_buf, id_smem, local_sem.at[0])
        to_smem.start()
        to_smem.wait()

    def piece(t):
        hops = (4, 3) if t % 2 == 0 else (3, 4)
        lanes = pl.ds(t * width, width)
        flying, shared = {}, []
        state = {}

        def hop_send(way, hop):
            slot = (z - (hop - 1) + NZ) % NZ if way == 0 else (z + (hop - 1)) % NZ
            flying[way] = send(columns[t].at[core, slot], columns[t].at[core, slot],
                               z_send.at[t, way, hop - 1], z_recv.at[t, way, hop - 1],
                               device(z_to=step(z, way, NZ)))

        def share(slot, index):
            shared.append(send(columns[t].at[core, slot], columns[t].at[core, slot],
                               c_send.at[t, index], c_recv.at[t, index], sibling))

        def begin():
            for way in range(2):
                hop_send(way, 1)
            share(z, 0)
            receivers(zl)

        def hop_stage(hop):
            def run():
                for way in range(2):
                    if hop <= hops[way]:
                        flying[way].wait_recv()
                        if hop < hops[way]:
                            hop_send(way, hop + 1)
                        share((z - hop + NZ) % NZ if way == 0 else (z + hop) % NZ, hop + way * hops[0])
                if hop < ZL:
                    receivers(jnp.where(zl == ZL - 1, ZL - 1 - hop, (zl + hop) % ZL))
            return run

        def ring_copy(way, src_ref, dst_ref):
            return pltpu.make_async_remote_copy(
                src_ref=src_ref, dst_ref=dst_ref, send_sem=r_send.at[t, way], recv_sem=r_recv.at[t, way],
                device_id=device(y_to=step(y, way, NY)), device_id_type=MESH)

        def receivers(member):
            own, target = columns[t].at[core, zh * ZL + member], rcv_ref.at[member, y, :, lanes]
            for way in range(2):
                ring_copy(way, own, target).start()
            pltpu.make_async_copy(own, target, local_sem.at[1 + t]).start()

        def ring_whole(way):
            return ring_copy(way, columns[t].at[core, pl.ds(zh * ZL, ZL)], rcv_ref.at[:, y, :, lanes])

        def receivers_on():
            way = t % 2
            ring_whole(way).wait_recv()
            held = rcv_ref.at[:, step(y, 1 - way, NY), :, lanes]
            state["on"] = send(held, held, r_send.at[t, 2], r_recv.at[t, 2], device(y_to=step(y, way, NY)))

        def pick():
            if t == 0:
                ids_ready()
            for copy in shared:
                copy.wait_recv()

            for y_of in range(NY):
                block = id_smem[y_of, core, 0]
                group = block // 2
                slot = (group // (NC * NX)) * ZL + (block % 2) * 2
                for p in range(2):
                    def take(q, h):
                        start = pl.multiple_of(q * part + h * half, half)
                        return columns[t][group % NC, slot + p, :, pl.ds(start, half)]

                    for h in range(2):
                        first[t][h, y_of, p] = take((x + 2) % NX, h)
                        landed[t][4 + h, y_of, p] = take(x, h)
                        mixed[t][h, 0, y_of, p] = take(step(x, h, NX), h)
                        second[t][h, 1, y_of, p] = take(step(x, h, NX), 1 - h)
            state["x1"] = [send(first[t].at[way], mixed[t].at[way, 1], x_send.at[t, way], x_recv.at[t, way],
                                device(x_to=step(x, way, NX))) for way in range(2)]

        def blend():
            for copy in state["x1"]:
                copy.wait_recv()
            state["x2"] = []
            for way in range(2):
                for y_of in range(NY):
                    root = (id_smem[y_of, core, 0] // (2 * NC)) % NX
                    other = jnp.where(root == step(x, 1 - way, NX), 1, 0)
                    second[t][way, 0, y_of] = mixed[t][way, other, y_of]
                state["x2"].append(send(second[t].at[way], landed[t].at[pl.ds(2 * way, 2)],
                                        x_send.at[t, 2 + way], x_recv.at[t, 2 + way],
                                        device(x_to=step(x, way, NX))))

        def choose():
            for copy in state["x2"]:
                copy.wait_recv()
            for y_of in range(NY):
                root = (id_smem[y_of, core, 0] // (2 * NC)) % NX
                away = (root - x + NX) % NX
                low = jnp.where(away == 0, 4, jnp.where(away == 1, 3, 0))
                high = jnp.where(away == 0, 5, jnp.where(away == 3, 1, 2))
                chosen[t][y_of, :, :, :half] = landed[t][low, y_of]
                chosen[t][y_of, :, :, half:] = landed[t][high, y_of]
            state["y"] = [send(chosen[t].at[(y + d) % NY], merged[t].at[:, y], y_send.at[t, d - 1],
                               y_recv.at[t, d - 1], device(y_to=(y + d) % NY)) for d in range(1, NY)]
            for p in range(2):
                merged[t][p, y] = chosen[t][y, p]

        def spread():
            for copy in state["y"]:
                copy.wait_recv()
            place = src_ref.at[core, :, :, :, pl.ds(t * width + x * part, part)]
            state["g1"] = [send(merged[t], place, g_send.at[t, way], g_recv.at[t, way],
                                device(x_to=step(x, way, NX))) for way in range(2)]
            copy = pltpu.make_async_copy(merged[t], place, local_sem.at[1 + PIECES + t])
            copy.start()
            state["own"] = copy

        def spread_on():
            state["g2"] = []
            for way in range(2):
                state["g1"][way].wait_recv()
                start = t * width + step(x, 1 - way, NX) * part + way * half
                held = src_ref.at[core, :, :, :, pl.ds(pl.multiple_of(start, half), half)]
                state["g2"].append(send(held, held, g_send.at[t, 2 + way], g_recv.at[t, 2 + way],
                                        device(x_to=step(x, way, NX))))

        def twin():
            for copy in state["g2"]:
                copy.wait_recv()
            state["own"].wait()
            whole = src_ref.at[core, :, :, :, lanes]
            state["twin"] = send(whole, whole, e_send.at[t], e_recv.at[t], sibling)

        def receivers_done():
            ring_whole(1 - t % 2).wait_recv()
            state["on"].wait_recv()
            for way in range(2):
                ring_whole(way).wait_send()
            pltpu.make_async_copy(columns[t].at[core, pl.ds(zh * ZL, ZL)], rcv_ref.at[:, y, :, lanes],
                                  local_sem.at[1 + t]).wait()

        def finish():
            state["twin"].wait_recv()
            held = src_ref.at[:, :, :, :, lanes]
            state["out"] = pltpu.make_async_copy(held, src_out.at[:, :, :, :, lanes], local_sem.at[1 + 2 * PIECES + t])
            state["out"].start()

        def end():
            state["out"].wait()

        return [begin] + [hop_stage(hop) for hop in range(1, NZ // 2 + 1)] + [
            pick, receivers_on, blend, choose, receivers_done, spread, spread_on, twin, finish, end]

    taps, count = spec_ref.shape[1], off_ref.shape[0]
    stored = []

    def to_spec(f, lane_half, values):
        spec_ref[f, :, lane_half * LANES:(lane_half + 1) * LANES] = values

    def windows_part(k, parts):
        windows(k * count // parts, (k + 1) * count // parts, 4, off_ref, dft_ref,
                lambda span: rcv_ref[:, :, :, span].reshape(ZL * NY * shard, SPAN), wide)

    def narrow_part(k, parts):
        size = BINS // parts
        narrow(k * size, (k + 1) * size, taps, wide, to_spec)
        piece_of = pl.ds(k * size, size)
        copy = pltpu.make_async_copy(spec_ref.at[piece_of], spec_out.at[piece_of],
                                     local_sem.at[1 + 3 * PIECES + k])
        copy.start()
        stored.append(copy)

    stages = [piece(t) for t in range(PIECES)]
    for slot in range(len(stages[0])):
        for t in range(PIECES):
            stages[t][slot]()
            late = slot - (len(stages[0]) - 5)
            if late in (0, 1):
                windows_part(late * PIECES + t, 2 * PIECES)
            if late == 2:
                narrow_part(t, PIECES)
    for copy in stored:
        copy.wait()
    for copy in sent:
        copy.wait_send()


def gather(records, live_mask, offsets, block_ids, dft):
    shard, total = records.shape
    width = total // PIECES
    part = width // NX
    half = part // 2
    turns = block_ids.shape[0]
    taps = 2 * offsets.shape[0]
    rcv_total = ZL * NY * shard
    dma = pltpu.SemaphoreType.DMA
    vmem = pl.BlockSpec(memory_space=pltpu.VMEM)
    smem = pl.BlockSpec(memory_space=pltpu.SMEM)
    hbm = pl.BlockSpec(memory_space=pl.ANY)
    buffers = [
        (NC, NZ, shard, width),
        (2, NY, 2, shard, half),
        (2, 2, NY, 2, shard, half),
        (2, 2, NY, 2, shard, half),
        (6, NY, 2, shard, half),
        (NY, 2, shard, part),
        (2, NY, shard, part),
    ]
    counts = [(PIECES, 2, 4), (PIECES, NZ), (PIECES, 4), (PIECES, 3), (PIECES, 4), (PIECES,),
              (PIECES, 3), (NY - 1,)]
    src_shape = (turns, 2, NY, shard, total)
    spec, src = pl.pallas_call(
        gather_kernel,
        name="gather",
        in_specs=[smem] * 3 + [vmem] * 2,
        out_specs=[hbm] * 2,
        out_shape=[
            jax.ShapeDtypeStruct((BINS, taps, rcv_total), records.dtype),
            jax.ShapeDtypeStruct(src_shape, records.dtype),
        ],
        scratch_shapes=(
            [
                pltpu.VMEM((ZL, NY, shard, total), records.dtype),
                pltpu.VMEM(src_shape, records.dtype),
                pltpu.VMEM((BINS, taps, rcv_total), records.dtype),
                pltpu.VMEM((2, BINS * STRIDE, LANES), jnp.float32),
            ]
            + [pltpu.VMEM(shape, records.dtype) for shape in buffers for _ in range(PIECES)]
            + [pltpu.VMEM((NY, 8, LANES), jnp.int32), pltpu.SMEM((NY, 8, LANES), jnp.int32)]
            + [dma(shape) for shape in counts for _ in range(2)]
            + [dma((1 + 4 * PIECES,))]
        ),
        compiler_params=pltpu.CompilerParams(
            collective_id=0, has_side_effects=True, vmem_limit_bytes=56 * 1024 * 1024),
    )(offsets, live_mask, block_ids, dft, records)
    return spec, src.reshape(-1, total)


def local(records, live_mask, offsets, block_ids):
    dft, padded, lag = tables(offsets.shape[0])
    block_ids = block_ids.reshape(-1)
    spec, src = gather(records, live_mask, offsets, block_ids, padded)
    return compute(offsets, block_ids, dft, lag, spec, src)


def solution(mesh):
    in_specs = (P(("rcv", "src"), None), P(("rcv", "src")), P(), P(None, "src"))
    out_specs = P(None, None, "src", "rcv")
    return jax.shard_map(local, mesh=mesh, in_specs=in_specs, out_specs=out_specs, check_vma=False)
```

```python
import jax
import jax.numpy as jnp
import numpy as np
from jax import lax
from jax.experimental import pallas as pl
from jax.experimental.pallas import tpu as pltpu
from jax.sharding import PartitionSpec as P

L = 256
SB = 128
LAGS = 76
LAGP = 80
BINS = L // 2
LANES = 128
SPAN = L + LANES
STRIDE = 132
GROUP = 64
LAST = (8192 - SPAN) // LANES
ROWS = 68


def tables(win_count):
    sample_axis = np.arange(L, dtype=np.float32)
    bin_axis = np.arange(BINS, dtype=np.float32)
    two_pi = np.float32(2.0 * np.pi)
    phases = two_pi * sample_axis[:, None] * bin_axis[None, :] / np.float32(L)
    taper = np.float32(0.5) - np.float32(0.5) * np.cos(two_pi * sample_axis / np.float32(L))
    dft = np.concatenate([taper[:, None] * np.cos(phases), -taper[:, None] * np.sin(phases)], axis=1)
    dft = dft.astype(jnp.bfloat16).astype(np.float32)
    shifted = np.zeros((L, SPAN), np.float32)
    shifted[:, :L] = dft.T
    lag_axis = np.arange(LAGS, dtype=np.float32)
    weights = np.where(bin_axis == 0, 1.0, 2.0).astype(np.float32)
    lag = (
        weights[:, None]
        * np.cos(two_pi * bin_axis[:, None] * lag_axis[None, :] / np.float32(L))
        * np.float32(2.0 / (win_count * L))
    )
    lag_t = np.zeros((LAGP, BINS), np.float32)
    lag_t[:LAGS] = lag.T
    padded = np.zeros((2, L + 2 * LANES, BINS), np.float32)
    padded[:, LANES:LANES + L] = dft.reshape(L, 2, BINS).transpose(1, 0, 2)
    return shifted, padded, lag_t.astype(jnp.bfloat16)


def windows(begin, end, unroll, off_ref, dft_ref, load, wide):
    win_count = off_ref.shape[0]

    @pl.loop(begin, end, unroll=unroll)
    def _(w):
        first = off_ref[w]
        base = jnp.minimum(first // LANES, LAST)
        samples = load(pl.ds(base * LANES, SPAN))
        if dft_ref.shape[0] == L:
            table = pltpu.roll(dft_ref[...], first - base * LANES, 1).astype(jnp.bfloat16)
            value = lax.dot_general(table, samples, (((1,), (1,)), ((), ())),
                                    preferred_element_type=jnp.float32)
            values = [value[part * BINS:(part + 1) * BINS] for part in range(2)]
        else:
            tables_t = [dft_ref[part, pl.ds(LANES - first + base * LANES, SPAN), :].astype(jnp.bfloat16)
                        for part in range(2)]
            values = [lax.dot_general(table, samples, (((0,), (1,)), ((), ())),
                                      preferred_element_type=jnp.float32) for table in tables_t]
        for half in range(2):
            for part in range(2):
                wide[half, pl.ds(part * win_count + w, BINS, stride=STRIDE), :] = (
                    values[part][:, half * LANES:(half + 1) * LANES])


def narrow(begin, end, taps, wide, store):
    @pl.loop(begin, end, unroll=8)
    def _(f):
        for half in range(2):
            rows = wide[half, pl.ds(pl.multiple_of(f * STRIDE, 4), taps), :]
            store(f, half, rows.astype(jnp.bfloat16))


def compute_kernel(off_ref, ids_ref, dft_ref, lag_ref, spec_ref, src_ref, out_ref,
                   spec_rcv, spec_src, wide, lagged, spec_sem):
    turn, group = pl.program_id(0), pl.program_id(1)
    win_count = off_ref.shape[0]
    taps = 2 * win_count
    rcv_first = lax.axis_index("rcv") * spec_rcv.shape[2]
    fetch = pltpu.make_async_copy(spec_ref, spec_rcv, spec_sem)

    @pl.when((turn == 0) & (group == 0))
    def _():
        fetch.start()

        windows(0, win_count, 16, off_ref, dft_ref, lambda span: src_ref[:, span], spec_src)
        fetch.wait()

    @pl.when(group == 0)
    def _():
        @pl.loop(0, BINS, unroll=64)
        def _(f):
            source = spec_src[turn, pl.ds(pl.multiple_of(f * STRIDE, 4), taps), :].astype(jnp.bfloat16)
            value = lax.dot_general(source, spec_rcv[f], (((0,), (0,)), ((), ())),
                                    preferred_element_type=jnp.float32)
            for half in range(2):
                wide[half, pl.ds(f, SB, stride=STRIDE), :] = value[:, half * LANES:(half + 1) * LANES]

    for s in range(GROUP):
        begin = pl.multiple_of((group * GROUP + s) * STRIDE, 4)
        cross = jnp.concatenate(
            [wide[half, pl.ds(begin, BINS), :].astype(jnp.bfloat16) for half in range(2)], axis=1)
        value = jnp.dot(lag_ref[...], cross, preferred_element_type=jnp.float32)
        for half in range(2):
            lagged[half, pl.ds(s, LAGP, stride=ROWS), :] = value[:, half * LANES:(half + 1) * LANES]
    src_chan = ids_ref[turn] * SB + group * GROUP + lax.broadcasted_iota(jnp.int32, (GROUP, LANES), 0)
    for half in range(2):
        rcv_chan = rcv_first + half * LANES + lax.broadcasted_iota(jnp.int32, (GROUP, LANES), 1)
        apart = src_chan != rcv_chan
        for lag in range(LAGS):
            value = lagged[half, lag * ROWS:lag * ROWS + GROUP, :]
            out_ref[0, lag, :, half * LANES:(half + 1) * LANES] = (
                jnp.where(apart, value, 0.0).astype(jnp.bfloat16))


def compute(offsets, block_ids, dft, lag, spec, src):
    win_count = offsets.shape[0]
    turns = block_ids.shape[0]
    bins, taps, rcv_total = spec.shape
    whole = lambda shape: pl.BlockSpec(shape, lambda t, g, *_: (0,) * len(shape), pipeline_mode=pl.Buffered(1))
    return pl.pallas_call(
        compute_kernel,
        name="correlate",
        grid_spec=pltpu.PrefetchScalarGridSpec(
            num_scalar_prefetch=2,
            grid=(turns, SB // GROUP),
            in_specs=[whole(dft.shape), whole(lag.shape), pl.BlockSpec(memory_space=pl.ANY), whole(src.shape)],
            out_specs=pl.BlockSpec((1, LAGS, GROUP, rcv_total), lambda t, g, *_: (t, 0, g, 0)),
            scratch_shapes=[
                pltpu.VMEM((bins, taps, rcv_total), jnp.bfloat16),
                pltpu.VMEM((turns, BINS * STRIDE, SB), jnp.float32),
                pltpu.VMEM((2, BINS * STRIDE, LANES), jnp.float32),
                pltpu.VMEM((2, LAGP * ROWS, LANES), jnp.float32),
                pltpu.SemaphoreType.DMA,
            ],
        ),
        out_shape=jax.ShapeDtypeStruct((turns, LAGS, SB, rcv_total), jnp.bfloat16),
        compiler_params=pltpu.CompilerParams(vmem_limit_bytes=60 * 1024 * 1024),
    )(offsets, block_ids, dft, lag, spec, src)


NX, NY, NZ, NC = 4, 4, 8, 2
ZL = NZ // 2
PIECES = 4
OFFSETS = (0, 0, 0, 0)
MESH = pl.DeviceIdType.MESH


def gather_kernel(off_ref, live_ref, ids_ref, dft_ref, rec_ref, spec_out, src_out, rcv_ref, src_ref, spec_ref,
                  wide, *scratch):
    columns, first, mixed, second, landed, chosen, merged = (
        scratch[i * PIECES:(i + 1) * PIECES] for i in range(7))
    (id_buf, id_smem, z_send, z_recv, c_send, c_recv, x_send, x_recv, y_send, y_recv,
     g_send, g_recv, e_send, e_recv, r_send, r_recv, i_send, i_recv,
     local_sem) = scratch[7 * PIECES:]
    shard, total = rec_ref.shape
    width = total // PIECES
    part = width // NX
    half = part // 2

    src, rcv = lax.axis_index("src"), lax.axis_index("rcv")
    y, zl = src % NY, src // NY
    core, x, zh = rcv % NC, (rcv // NC) % NX, rcv // (NC * NX)
    z = zh * ZL + zl

    def device(x_to=x, y_to=y, z_to=z, core_to=core):
        return {"src": (z_to % ZL) * NY + y_to,
                "rcv": ((z_to // ZL) * NX + x_to) * NC + core_to}

    sent = []

    def send(src_ref, dst_ref, send_sem, recv_sem, to):
        copy = pltpu.make_async_remote_copy(
            src_ref=src_ref, dst_ref=dst_ref, send_sem=send_sem, recv_sem=recv_sem,
            device_id=to, device_id_type=MESH)
        copy.start()
        sent.append(copy)
        return copy

    def step(position, way, count):
        return (position + 1) % count if way == 0 else (position + count - 1) % count

    sibling = device(core_to=1 - core)
    barrier = pltpu.get_barrier_semaphore()
    peers = [device(z_to=step(z, way, NZ)) for way in range(2)] + [sibling]
    peers += [device(x_to=step(x, way, NX)) for way in range(2)]
    peers += [device(y_to=(y + d) % NY) for d in range(1, NY)]
    for peer in peers:
        pl.semaphore_signal(barrier, inc=1, device_id=peer, device_id_type=MESH)

    rows = lax.broadcasted_iota(jnp.int32, (shard, LANES), 0)
    live = jnp.zeros((shard, LANES), jnp.float32)
    for channel in range(shard):
        live = jnp.where(rows == channel, live_ref[channel].astype(jnp.float32), live)
    live = live[:, :1].astype(rec_ref.dtype)
    for t in range(PIECES):
        columns[t][core, z] = rec_ref[:, t * width:(t + 1) * width] * live
    id_buf[y] = jnp.where(lax.broadcasted_iota(jnp.int32, (8, LANES), 0) == 0, ids_ref[0], ids_ref[1])
    pl.semaphore_wait(barrier, len(peers))

    ids = [send(id_buf.at[y], id_buf.at[y], i_send.at[d - 1], i_recv.at[d - 1],
                device(y_to=(y + d) % NY)) for d in range(1, NY)]

    def ids_ready():
        for copy in ids:
            copy.wait_recv()
        to_smem = pltpu.make_async_copy(id_buf, id_smem, local_sem.at[0])
        to_smem.start()
        to_smem.wait()

    def piece(t):
        hops = (4, 3) if t % 2 == 0 else (3, 4)
        lanes = pl.ds(t * width, width)
        flying, shared = {}, []
        state = {}

        def hop_send(way, hop):
            slot = (z - (hop - 1) + NZ) % NZ if way == 0 else (z + (hop - 1)) % NZ
            flying[way] = send(columns[t].at[core, slot], columns[t].at[core, slot],
                               z_send.at[t, way, hop - 1], z_recv.at[t, way, hop - 1],
                               device(z_to=step(z, way, NZ)))

        def share(slot, index):
            shared.append(send(columns[t].at[core, slot], columns[t].at[core, slot],
                               c_send.at[t, index], c_recv.at[t, index], sibling))

        def begin():
            for way in range(2):
                hop_send(way, 1)
            share(z, 0)
            receivers(zl)

        def hop_stage(hop):
            def run():
                for way in range(2):
                    if hop <= hops[way]:
                        flying[way].wait_recv()
                        if hop < hops[way]:
                            hop_send(way, hop + 1)
                        share((z - hop + NZ) % NZ if way == 0 else (z + hop) % NZ, hop + way * hops[0])
                if hop < ZL:
                    receivers(jnp.where(zl == ZL - 1, ZL - 1 - hop, (zl + hop) % ZL))
            return run

        def ring_copy(way, src_ref, dst_ref):
            return pltpu.make_async_remote_copy(
                src_ref=src_ref, dst_ref=dst_ref, send_sem=r_send.at[t, way], recv_sem=r_recv.at[t, way],
                device_id=device(y_to=step(y, way, NY)), device_id_type=MESH)

        def receivers(member):
            own, target = columns[t].at[core, zh * ZL + member], rcv_ref.at[member, y, :, lanes]
            for way in range(2):
                ring_copy(way, own, target).start()
            pltpu.make_async_copy(own, target, local_sem.at[1 + t]).start()

        def ring_whole(way):
            return ring_copy(way, columns[t].at[core, pl.ds(zh * ZL, ZL)], rcv_ref.at[:, y, :, lanes])

        def receivers_on():
            way = t % 2
            ring_whole(way).wait_recv()
            held = rcv_ref.at[:, step(y, 1 - way, NY), :, lanes]
            state["on"] = send(held, held, r_send.at[t, 2], r_recv.at[t, 2], device(y_to=step(y, way, NY)))

        def pick():
            if t == 0:
                ids_ready()
            for copy in shared:
                copy.wait_recv()

            for y_of in range(NY):
                block = id_smem[y_of, core, 0]
                group = block // 2
                slot = (group // (NC * NX)) * ZL + (block % 2) * 2
                for p in range(2):
                    def take(q, h):
                        start = pl.multiple_of(q * part + h * half, half)
                        return columns[t][group % NC, slot + p, :, pl.ds(start, half)]

                    for h in range(2):
                        first[t][h, y_of, p] = take((x + 2) % NX, h)
                        landed[t][4 + h, y_of, p] = take(x, h)
                        mixed[t][h, 0, y_of, p] = take(step(x, h, NX), h)
                        second[t][h, 1, y_of, p] = take(step(x, h, NX), 1 - h)
            state["x1"] = [send(first[t].at[way], mixed[t].at[way, 1], x_send.at[t, way], x_recv.at[t, way],
                                device(x_to=step(x, way, NX))) for way in range(2)]

        def blend():
            for copy in state["x1"]:
                copy.wait_recv()
            state["x2"] = []
            for way in range(2):
                for y_of in range(NY):
                    root = (id_smem[y_of, core, 0] // (2 * NC)) % NX
                    other = jnp.where(root == step(x, 1 - way, NX), 1, 0)
                    second[t][way, 0, y_of] = mixed[t][way, other, y_of]
                state["x2"].append(send(second[t].at[way], landed[t].at[pl.ds(2 * way, 2)],
                                        x_send.at[t, 2 + way], x_recv.at[t, 2 + way],
                                        device(x_to=step(x, way, NX))))

        def choose():
            for copy in state["x2"]:
                copy.wait_recv()
            for y_of in range(NY):
                root = (id_smem[y_of, core, 0] // (2 * NC)) % NX
                away = (root - x + NX) % NX
                low = jnp.where(away == 0, 4, jnp.where(away == 1, 3, 0))
                high = jnp.where(away == 0, 5, jnp.where(away == 3, 1, 2))
                chosen[t][y_of, :, :, :half] = landed[t][low, y_of]
                chosen[t][y_of, :, :, half:] = landed[t][high, y_of]
            state["y"] = [send(chosen[t].at[(y + d) % NY], merged[t].at[:, y], y_send.at[t, d - 1],
                               y_recv.at[t, d - 1], device(y_to=(y + d) % NY)) for d in range(1, NY)]
            for p in range(2):
                merged[t][p, y] = chosen[t][y, p]

        def spread():
            for copy in state["y"]:
                copy.wait_recv()
            place = src_ref.at[core, :, :, :, pl.ds(t * width + x * part, part)]
            state["g1"] = [send(merged[t], place, g_send.at[t, way], g_recv.at[t, way],
                                device(x_to=step(x, way, NX))) for way in range(2)]
            copy = pltpu.make_async_copy(merged[t], place, local_sem.at[1 + PIECES + t])
            copy.start()
            state["own"] = copy

        def spread_on():
            state["g2"] = []
            for way in range(2):
                state["g1"][way].wait_recv()
                start = t * width + step(x, 1 - way, NX) * part + way * half
                held = src_ref.at[core, :, :, :, pl.ds(pl.multiple_of(start, half), half)]
                state["g2"].append(send(held, held, g_send.at[t, 2 + way], g_recv.at[t, 2 + way],
                                        device(x_to=step(x, way, NX))))

        def twin():
            for copy in state["g2"]:
                copy.wait_recv()
            state["own"].wait()
            whole = src_ref.at[core, :, :, :, lanes]
            state["twin"] = send(whole, whole, e_send.at[t], e_recv.at[t], sibling)

        def receivers_done():
            ring_whole(1 - t % 2).wait_recv()
            state["on"].wait_recv()
            for way in range(2):
                ring_whole(way).wait_send()
            pltpu.make_async_copy(columns[t].at[core, pl.ds(zh * ZL, ZL)], rcv_ref.at[:, y, :, lanes],
                                  local_sem.at[1 + t]).wait()

        def finish():
            state["twin"].wait_recv()
            held = src_ref.at[:, :, :, :, lanes]
            state["out"] = pltpu.make_async_copy(held, src_out.at[:, :, :, :, lanes], local_sem.at[1 + 2 * PIECES + t])
            state["out"].start()

        def end():
            state["out"].wait()

        return [begin] + [hop_stage(hop) for hop in range(1, NZ // 2 + 1)] + [
            pick, receivers_on, blend, choose, receivers_done, spread, spread_on, twin, finish, end]

    taps, count = spec_ref.shape[1], off_ref.shape[0]
    stored = []

    def to_spec(f, lane_half, values):
        spec_ref[f, :, lane_half * LANES:(lane_half + 1) * LANES] = values

    def windows_part(k, parts):
        windows(k * count // parts, (k + 1) * count // parts, 4, off_ref, dft_ref,
                lambda span: rcv_ref[:, :, :, span].reshape(ZL * NY * shard, SPAN), wide)

    def narrow_part(k, parts):
        size = BINS // parts
        narrow(k * size, (k + 1) * size, taps, wide, to_spec)
        piece_of = pl.ds(k * size, size)
        copy = pltpu.make_async_copy(spec_ref.at[piece_of], spec_out.at[piece_of],
                                     local_sem.at[1 + 3 * PIECES + k])
        copy.start()
        stored.append(copy)

    stages = [piece(t) for t in range(PIECES)]
    for slot in range(len(stages[0])):
        for t in range(PIECES):
            stages[t][slot]()
            late = slot - (len(stages[0]) - 5)
            if late in (0, 1):
                windows_part(late * PIECES + t, 2 * PIECES)
            if late == 2:
                narrow_part(t, PIECES)
    for copy in stored:
        copy.wait()
    for copy in sent:
        copy.wait_send()


def gather(records, live_mask, offsets, block_ids, dft):
    shard, total = records.shape
    width = total // PIECES
    part = width // NX
    half = part // 2
    turns = block_ids.shape[0]
    taps = 2 * offsets.shape[0]
    rcv_total = ZL * NY * shard
    dma = pltpu.SemaphoreType.DMA
    vmem = pl.BlockSpec(memory_space=pltpu.VMEM)
    smem = pl.BlockSpec(memory_space=pltpu.SMEM)
    hbm = pl.BlockSpec(memory_space=pl.ANY)
    buffers = [
        (NC, NZ, shard, width),
        (2, NY, 2, shard, half),
        (2, 2, NY, 2, shard, half),
        (2, 2, NY, 2, shard, half),
        (6, NY, 2, shard, half),
        (NY, 2, shard, part),
        (2, NY, shard, part),
    ]
    counts = [(PIECES, 2, 4), (PIECES, NZ), (PIECES, 4), (PIECES, 3), (PIECES, 4), (PIECES,),
              (PIECES, 3), (NY - 1,)]
    src_shape = (turns, 2, NY, shard, total)
    spec, src = pl.pallas_call(
        gather_kernel,
        name="gather",
        in_specs=[smem] * 3 + [vmem] * 2,
        out_specs=[hbm] * 2,
        out_shape=[
            jax.ShapeDtypeStruct((BINS, taps, rcv_total), records.dtype),
            jax.ShapeDtypeStruct(src_shape, records.dtype),
        ],
        scratch_shapes=(
            [
                pltpu.VMEM((ZL, NY, shard, total), records.dtype),
                pltpu.VMEM(src_shape, records.dtype),
                pltpu.VMEM((BINS, taps, rcv_total), records.dtype),
                pltpu.VMEM((2, BINS * STRIDE, LANES), jnp.float32),
            ]
            + [pltpu.VMEM(shape, records.dtype) for shape in buffers for _ in range(PIECES)]
            + [pltpu.VMEM((NY, 8, LANES), jnp.int32), pltpu.SMEM((NY, 8, LANES), jnp.int32)]
            + [dma(shape) for shape in counts for _ in range(2)]
            + [dma((1 + 4 * PIECES,))]
        ),
        compiler_params=pltpu.CompilerParams(
            collective_id=0, has_side_effects=True, vmem_limit_bytes=56 * 1024 * 1024),
    )(offsets, live_mask, block_ids, dft, records)
    return spec, src.reshape(-1, total)


def local(records, live_mask, offsets, block_ids):
    dft, padded, lag = tables(offsets.shape[0])
    block_ids = block_ids.reshape(-1)
    spec, src = gather(records, live_mask, offsets, block_ids, padded)
    return compute(offsets, block_ids, dft, lag, spec, src)


def solution(mesh):
    in_specs = (P(("rcv", "src"), None), P(("rcv", "src")), P(), P(None, "src"))
    out_specs = P(None, None, "src", "rcv")
    return jax.shard_map(local, mesh=mesh, in_specs=in_specs, out_specs=out_specs, check_vma=False)
```
